32 devices in a mesh: dp: 4 (over x, core), fsdp: 8 (over z, y).
Axes of the slice: x: 2, y: 2, z: 4, core: 2. Of those that a mesh axis runs over, the one named last changes fastest.
Arguments:
- mel_clips: bfloat16 [640, 256, 512], P(('dp', 'fsdp')), may hold values from -6 to 6
- live_counts: int32 [32, 4], P(('dp', 'fsdp')), may hold values from 1 to 5, as said below
- conv_weight: bfloat16 [512, 7], P(('dp', 'fsdp')), may hold values from -2 to 2
- conv_bias: bfloat16 [512], P(('dp', 'fsdp')), may hold values from -3 to 3
- norm_gain: bfloat16 [512], P(('dp', 'fsdp')), may hold values from 0.25 to 1.75
- norm_shift: bfloat16 [512], P(('dp', 'fsdp')), may hold values from -2 to 2
- in_weight: bfloat16 [512, 1536], P(('dp', 'fsdp')), may hold values from -0.25 to 0.25
- in_bias: bfloat16 [1536], P(('dp', 'fsdp')), may hold values from -2 to 2
- out_weight: bfloat16 [1536, 512], P(('dp', 'fsdp')), may hold values from -0.3125 to 0.3125
- out_bias: bfloat16 [512], P(('dp', 'fsdp')), may hold values from -2 to 2
- layer_scale: bfloat16 [512], P(('dp', 'fsdp')), may hold values from 0.29882812 to 1.1953125
- cotangent: bfloat16 [640, 256, 512], P(('dp', 'fsdp')), may hold values from -6 to 6
Outputs:
- block_out: bfloat16 [640, 256, 512], P(('dp', 'fsdp'))
- grad_clips: bfloat16 [640, 256, 512], P(('dp', 'fsdp'))
- grad_conv_weight: float32 [512, 7], P(('dp', 'fsdp'))
- grad_conv_bias: float32 [512], P(('dp', 'fsdp'))
- grad_norm_gain: float32 [512], P(('dp', 'fsdp'))
- grad_norm_shift: float32 [512], P(('dp', 'fsdp'))
- grad_in_weight: float32 [512, 1536], P(('dp', 'fsdp'))
- grad_in_bias: float32 [1536], P(('dp', 'fsdp'))
- grad_out_weight: float32 [1536, 512], P(('dp', 'fsdp'))
- grad_out_bias: float32 [512], P(('dp', 'fsdp'))
- grad_layer_scale: float32 [512], P(('dp', 'fsdp'))
The draws below stay inside these ranges and needn't reach their ends.
Inputs may be any that keep to these rules, and one draw needn't show every extreme that they name: Slot s of micro-batch m on device d holds a live clip when s < live_counts[d, m]; some device has all 5 slots live in some micro-batch, and some device only one.
All inputs are finite; a program needn't handle non-finite values.
Results may differ from the reference program's by a relative error of at most 0.0063.
Values may be sent and summed in bfloat16 or wider, within the bound.
A program may use at most 256 MiB of HBM per device.

```python
import jax
import jax.numpy as jnp
from jax import lax

C = 512
HID = 1536
KERNEL = 7
FRAMES = 256
MICRO = 4
SLOTS = 5
SHARDS = 32
CLIPS = 640


def draw_live_counts(key, part):
    entries = SHARDS * MICRO
    counts = jax.random.randint(jax.random.fold_in(key, 11), (entries,), 1, SLOTS + 1)
    picked = jax.random.randint(jax.random.fold_in(key, 12), (), 0, entries)
    second = (picked + 1 + jax.random.randint(jax.random.fold_in(key, 13), (), 0, entries - 1)) % entries
    counts = counts.at[picked].set(SLOTS).at[second].set(1)
    return counts.reshape(SHARDS, MICRO).astype(jnp.int32)


def spiked(array, own_key, source, target, parts, factor):
    def block_of(dim):
        return (jnp.arange(array.shape[dim]) // (array.shape[dim] // parts)).reshape((-1,) + (1,) * (array.ndim - 1 - dim))

    near = jax.random.permutation(own_key, parts)[block_of(target)]
    other_side = (block_of(target) + parts // 2) % parts
    return jnp.where((block_of(source) == near) | (block_of(source) == other_side), factor * array, array)


def level_of(stream_key, extent, pieces, least, top_value):
    gain = 1.0
    for position, blocks in pieces:
        steps = jax.random.uniform(jax.random.fold_in(jax.random.fold_in(stream_key, 6), position), (blocks,), jnp.float32, least / len(pieces), top_value / len(pieces))
        gain = gain * jnp.repeat(jnp.exp(steps), extent[position] // blocks).reshape((-1,) + (1,) * (len(extent) - 1 - position))
    return gain


def scatter_about(stream_key, shape, width, most, split=(), held_as=jnp.bfloat16):
    gain = level_of(stream_key, shape, split, -0.22, 0.18) if split else 1.0
    values = jax.random.normal(stream_key, shape, jnp.float32) * width * gain
    return jnp.minimum(jnp.maximum(values, -most), most).astype(held_as)


def heavy_noise(rng, extent, deviation, limit, cuts, heavy, dtype=jnp.bfloat16):
    values = deviation * jax.random.normal(rng, extent, jnp.float32)
    if cuts:
        values = values * level_of(rng, extent, cuts, -0.22, 0.18)
    return jnp.clip(spiked(values, jax.random.fold_in(rng, 3), *heavy), -limit, limit).astype(dtype)


def setup_inputs(seed: int = 0) -> dict:
    keys = jax.random.split(jax.random.key(seed), 13)
    mel_clips = scatter_about(keys[0], (CLIPS, FRAMES, C), 1.0, 6.0, ((0, 32),))
    live_counts = draw_live_counts(jax.random.fold_in(keys[12], 71), 0)
    conv_weight = scatter_about(keys[2], (C, KERNEL), KERNEL ** -0.5, 2.0, ((0, 32),))
    conv_bias = scatter_about(keys[3], (C,), 0.5, 3.0, ((0, 32),))
    norm_gain = jnp.clip(1.0 + 0.15 * jax.random.normal(keys[4], (C,), jnp.float32), 0.25, 1.75).astype(jnp.bfloat16)
    norm_shift = scatter_about(keys[5], (C,), 0.3, 2.0, ((0, 32),))
    in_weight = scatter_about(keys[6], (C, HID), C ** -0.5, 0.25, ((0, 32),))
    in_bias = scatter_about(keys[7], (HID,), 0.3, 2.0, ((0, 32),))
    out_weight = scatter_about(keys[8], (HID, C), (HID // 4) ** -0.5, 0.3125, ((0, 32),))
    out_bias = scatter_about(keys[9], (C,), 0.3, 2.0, ((0, 32),))
    layer_scale = jnp.clip(0.29882812 + 0.8964844 * jax.random.uniform(keys[10], (C,), jnp.float32) ** level_of(keys[10], (C,), ((0, 32),), -0.2, 0.2), 0.29882812, 1.1953125).astype(jnp.bfloat16)
    cotangent = heavy_noise(keys[11], (CLIPS, FRAMES, C), 1.0, 6.0, ((0, 32),), (0, 2, 32, 2.75))
    return dict(mel_clips=mel_clips, live_counts=live_counts, conv_weight=conv_weight, conv_bias=conv_bias, norm_gain=norm_gain, norm_shift=norm_shift, in_weight=in_weight, in_bias=in_bias, out_weight=out_weight, out_bias=out_bias, layer_scale=layer_scale, cotangent=cotangent)


@jax.custom_vjp
def low(v):
    return lax.optimization_barrier(v.astype(jnp.bfloat16)).astype(jnp.float32)

@jax.custom_vjp
def low_back(v):
    return v

def low_keep(v):
    return (low(v), None)

def low_pass(kept, grad):
    return (grad,)

def back_keep(v):
    return (v, None)

def back_low(kept, grad):
    return (low(grad),)
low.defvjp(low_keep, low_pass)
low_back.defvjp(back_keep, back_low)

def conv_norm(mel_block, conv_weight, conv_bias, norm_gain, norm_shift):
    frames = mel_block.shape[1]
    margin = (KERNEL - 1) // 2
    padded = jnp.pad(mel_block, ((0, 0), (margin, margin), (0, 0)))
    mixed_sum = conv_bias + padded[:, 0:frames, :] * conv_weight[:, 0]
    for offset in range(1, KERNEL):
        mixed_sum = mixed_sum + padded[:, offset:offset + frames, :] * conv_weight[:, offset]
    center = mixed_sum - lax.optimization_barrier(jnp.mean(mixed_sum, axis=-1, keepdims=True))
    spread = lax.optimization_barrier(jnp.mean(center * center, axis=-1, keepdims=True))
    return center * lax.rsqrt(spread + 1e-06) * norm_gain + norm_shift

def forward(mel_block, live_mask, params):
    conv_weight, conv_bias, norm_gain, norm_shift, in_weight, in_bias, out_weight, out_bias, layer_scale = params
    normed = low(conv_norm(mel_block, conv_weight, conv_bias, norm_gain, norm_shift))
    tok_rows = normed.reshape(-1, normed.shape[-1])
    hidden = low_back(jnp.dot(tok_rows, in_weight, precision=lax.Precision.HIGHEST) + in_bias)
    active = low(jax.nn.gelu(hidden, approximate=False))
    output = low_back(jnp.dot(active, out_weight, precision=lax.Precision.HIGHEST) + out_bias)
    branch = output.reshape(mel_block.shape) * layer_scale * live_mask[:, None, None]
    return mel_block + branch

def reference(mel_clips, live_counts, conv_weight, conv_bias, norm_gain, norm_shift, in_weight, in_bias, out_weight, out_bias, layer_scale, cotangent):
    params = tuple((p.astype(jnp.float32) for p in (conv_weight, conv_bias, norm_gain, norm_shift, in_weight, in_bias, out_weight, out_bias, layer_scale)))
    blocks = SHARDS * MICRO
    clip_blocks = mel_clips.reshape(blocks, SLOTS, FRAMES, C)
    cot_blocks = cotangent.reshape(blocks, SLOTS, FRAMES, C)
    count_list = live_counts.reshape(blocks).astype(jnp.int32)

    def one_block(totals, inputs):
        mel_block, cot_block, count_now = inputs
        live_mask = (lax.iota(jnp.int32, SLOTS) < count_now).astype(jnp.float32)
        result, pullback = jax.vjp(lambda xin, pin: forward(xin, live_mask, pin), mel_block.astype(jnp.float32), params)
        grad_x, grad_params = pullback(cot_block.astype(jnp.float32))
        totals = tuple((a + b for a, b in zip(totals, grad_params)))
        return (totals, (result.astype(jnp.bfloat16), grad_x.astype(jnp.bfloat16)))
    zeros = tuple((jnp.zeros(p.shape, jnp.float32) for p in params))
    totals, (results, grads) = lax.scan(one_block, zeros, (clip_blocks, cot_blocks, count_list))
    block_out = results.reshape(CLIPS, FRAMES, C)
    grad_clips = grads.reshape(CLIPS, FRAMES, C)
    return (block_out, grad_clips, totals[0], totals[1], totals[2], totals[3], totals[4], totals[5], totals[6], totals[7], totals[8])
```

```python
from functools import partial
import jax
import jax.numpy as jnp
from jax import lax
from jax.experimental import pallas as pl
from jax.experimental.pallas import tpu as pltpu
from jax.sharding import PartitionSpec as P

F32 = jnp.float32
BF16 = jnp.bfloat16
PAD = 8
ROOT_HALF = 0.7071067811865476
LOG2E = 1.4426950408889634
INV_ROOT_2PI = 0.3989422804014327


def dot_nn(a, b):
    return lax.dot_general(a, b, (((1,), (0,)), ((), ())), preferred_element_type=F32)


def dot_nt(a, b):
    return lax.dot_general(a, b, (((1,), (1,)), ((), ())), preferred_element_type=F32)


def fold8(v):
    total = v[0:8]
    for r in range(8, v.shape[0], 8):
        total = total + v[r : r + 8]
    return total


def clip_kernel(
    live_ref,
    x_ref,
    dy_ref,
    w_in_ref,
    w_out_ref,
    rows_ref,
    ib_ref,
    out_ref,
    gx_ref,
    gin_ref,
    gout_ref,
    small_ref,
    gib_ref,
    xp,
    gm,
    xh,
    rs,
    nb,
    nbt,
    gob,
    gobt,
    ab,
    ghb,
    gn,
    acc_in,
    acc_out,
    acc_small,
    acc_ib,
    *,
    taps,
    hid_chunk,
    row_chunk,
):
    step = pl.program_id(0)
    frames, chans = xh.shape
    hid = ab.shape[1]
    margin = (taps - 1) // 2

    @pl.when(step == 0)
    def _():
        acc_in[...] = jnp.zeros_like(acc_in)
        acc_out[...] = jnp.zeros_like(acc_out)
        acc_small[...] = jnp.zeros_like(acc_small)
        acc_ib[...] = jnp.zeros_like(acc_ib)
        xp[0:PAD, :] = jnp.zeros((PAD, chans), F32)
        xp[PAD + frames :, :] = jnp.zeros((PAD, chans), F32)
        gm[0:PAD, :] = jnp.zeros((PAD, chans), F32)
        gm[PAD + frames :, :] = jnp.zeros((PAD, chans), F32)

    live = live_ref[step] != 0

    @pl.when(jnp.logical_not(live))
    def _():
        out_ref[...] = x_ref[...]
        gx_ref[...] = dy_ref[...]

    @pl.when(live)
    def _():
        def row(i):
            return rows_ref[i : i + 1, :]

        for r in range(0, frames, row_chunk):
            xp[PAD + r : PAD + r + row_chunk, :] = x_ref[0, r : r + row_chunk, :].astype(F32)
        for r in range(0, frames, row_chunk):
            base = PAD - margin + r
            mixed = row(taps) + xp[base : base + row_chunk, :] * row(0)
            for k in range(1, taps):
                mixed = mixed + xp[base + k : base + k + row_chunk, :] * row(k)
            center = mixed - jnp.mean(mixed, axis=-1, keepdims=True)
            var = jnp.mean(center * center, axis=-1, keepdims=True)
            inv = lax.rsqrt(var + 1e-06)
            xhat = center * inv
            xh[r : r + row_chunk, :] = xhat
            rs[r : r + row_chunk, :] = jnp.broadcast_to(inv, (row_chunk, 128))
            nb[r : r + row_chunk, :] = (xhat * row(taps + 1) + row(taps + 2)).astype(BF16)
            go = (dy_ref[0, r : r + row_chunk, :].astype(F32) * row(taps + 4)).astype(BF16)
            gob[r : r + row_chunk, :] = go
            acc_small[taps + 3, :, :] += fold8(go.astype(F32))
        nbt[...] = nb[...].T
        gobt[...] = gob[...].T

        for j in range(0, hid, hid_chunk):
            cols = slice(j, j + hid_chunk)
            h = dot_nn(nb[...], w_in_ref[:, cols]) + ib_ref[0:1, cols]
            u = h * ROOT_HALF
            cdf = 0.5 * lax.erf(u) + 0.5
            slope = cdf + h * (jnp.exp2(u * u * (-LOG2E)) * INV_ROOT_2PI)
            ab[:, cols] = (h * cdf).astype(BF16)
            ga = dot_nt(gob[...], w_out_ref[cols, :])
            gh = (ga * slope).astype(BF16)
            ghb[:, cols] = gh
            acc_ib[:, cols] += fold8(gh.astype(F32))
        gn[...] = dot_nt(ghb[...], w_in_ref[...])
        output = dot_nn(ab[...], w_out_ref[...]) + row(taps + 3)
        for r in range(0, frames, row_chunk):
            o = output[r : r + row_chunk, :]
            dy = dy_ref[0, r : r + row_chunk, :].astype(F32)
            acc_small[taps + 4, :, :] += fold8(dy * o)
            x = x_ref[0, r : r + row_chunk, :].astype(F32)
            out_ref[0, r : r + row_chunk, :] = (x + o * row(taps + 4)).astype(BF16)
        for j in range(0, hid, hid_chunk):
            cols = slice(j, j + hid_chunk)
            acc_out[:, cols] += dot_nn(gobt[...], ab[:, cols])
            acc_in[:, cols] += dot_nn(nbt[...], ghb[:, cols])

        for r in range(0, frames, row_chunk):
            g = gn[r : r + row_chunk, :]
            xhat = xh[r : r + row_chunk, :]
            gxh = g * xhat
            acc_small[taps + 2, :, :] += fold8(g)
            acc_small[taps + 1, :, :] += fold8(gxh)
            gg = g * row(taps + 1)
            m1 = jnp.mean(gg, axis=-1, keepdims=True)
            m2 = jnp.mean(gg * xhat, axis=-1, keepdims=True)
            gmix = rs[r : r + row_chunk, 0:1] * (gg - m1 - xhat * m2)
            acc_small[taps, :, :] += fold8(gmix)
            gm[PAD + r : PAD + r + row_chunk, :] = gmix
        for r in range(0, frames, row_chunk):
            base = PAD + margin + r
            x = xp[PAD + r : PAD + r + row_chunk, :]
            total = dy_ref[0, r : r + row_chunk, :].astype(F32)
            for k in range(taps):
                shifted = gm[base - k : base - k + row_chunk, :]
                total = total + shifted * row(k)
                acc_small[k, :, :] += fold8(shifted * x)
            gx_ref[0, r : r + row_chunk, :] = total.astype(BF16)

    @pl.when(step == pl.num_programs(0) - 1)
    def _():
        gin_ref[...] = acc_in[...].astype(gin_ref.dtype)
        for j in range(0, hid, 128):
            gout_ref[j : j + 128, :] = acc_out[:, j : j + 128].T.astype(gout_ref.dtype)
        small_ref[...] = acc_small[...]
        gib_ref[...] = acc_ib[...]


def clip_call(live, x, dy, w_in, w_out, rows, ib, taps, grad_dtype=F32):
    clips, frames, chans = x.shape
    hid = w_in.shape[1]
    clip_spec = pl.BlockSpec((1, frames, chans), lambda i, live: (i, 0, 0))
    whole = lambda shape: pl.BlockSpec(shape, lambda i, live: (0,) * len(shape), pipeline_mode=pl.Buffered(1))
    kinds = taps + 5
    return pl.pallas_call(
        partial(clip_kernel, taps=taps, hid_chunk=256, row_chunk=32),
        out_shape=(
            jax.ShapeDtypeStruct(x.shape, BF16),
            jax.ShapeDtypeStruct(x.shape, BF16),
            jax.ShapeDtypeStruct((chans, hid), grad_dtype),
            jax.ShapeDtypeStruct((hid, chans), grad_dtype),
            jax.ShapeDtypeStruct((kinds, 8, chans), F32),
            jax.ShapeDtypeStruct((8, hid), F32),
        ),
        grid_spec=pltpu.PrefetchScalarGridSpec(
            num_scalar_prefetch=1,
            grid=(clips,),
            in_specs=[
                clip_spec,
                clip_spec,
                whole((chans, hid)),
                whole((hid, chans)),
                whole(rows.shape),
                whole(ib.shape),
            ],
            out_specs=(
                clip_spec,
                clip_spec,
                whole((chans, hid)),
                whole((hid, chans)),
                whole((kinds, 8, chans)),
                whole((8, hid)),
            ),
            scratch_shapes=[
                pltpu.VMEM((frames + 2 * PAD, chans), F32),
                pltpu.VMEM((frames + 2 * PAD, chans), F32),
                pltpu.VMEM((frames, chans), F32),
                pltpu.VMEM((frames, 128), F32),
                pltpu.VMEM((frames, chans), BF16),
                pltpu.VMEM((chans, frames), BF16),
                pltpu.VMEM((frames, chans), BF16),
                pltpu.VMEM((chans, frames), BF16),
                pltpu.VMEM((frames, hid), BF16),
                pltpu.VMEM((frames, hid), BF16),
                pltpu.VMEM((frames, chans), F32),
                pltpu.VMEM((chans, hid), F32),
                pltpu.VMEM((chans, hid), F32),
                pltpu.VMEM((kinds, 8, chans), F32),
                pltpu.VMEM((8, hid), F32),
            ],
        ),
        compiler_params=pltpu.CompilerParams(vmem_limit_bytes=56 << 20),
        name="clips",
    )(live, x, dy, w_in, w_out, rows, ib)


def on_device(
    mel_clips,
    live_counts,
    conv_weight,
    conv_bias,
    norm_gain,
    norm_shift,
    in_weight,
    in_bias,
    out_weight,
    out_bias,
    layer_scale,
    cotangent,
):
    axes = ("dp", "fsdp")
    taps = conv_weight.shape[1]
    micro_count = live_counts.shape[1]
    slot_count = mel_clips.shape[0] // micro_count
    gather = partial(lax.all_gather, axis_name=axes, axis=0, tiled=True)
    scatter = partial(lax.psum_scatter, axis_name=axes, scatter_dimension=0, tiled=True)

    full_in = gather(in_weight)
    full_out = gather(out_weight)
    columns = jnp.stack([conv_bias, norm_gain, norm_shift, out_bias, layer_scale], axis=1)
    rows = gather(jnp.concatenate([conv_weight, columns], axis=1)).T.astype(F32)
    rows = jnp.pad(rows, ((0, 16 - rows.shape[0]), (0, 0)))
    bias_row = jnp.broadcast_to(gather(in_bias).astype(F32), (8, full_in.shape[1]))
    live = (lax.iota(jnp.int32, slot_count)[None, :] < live_counts[0][:, None]).astype(jnp.int32)

    block_out, grad_clips, grad_in, grad_out, small, grad_ib = clip_call(
        live.reshape(-1), mel_clips, cotangent, full_in, full_out, rows, bias_row, taps
    )
    small = scatter(jnp.sum(small, axis=1).T)
    return (
        block_out,
        grad_clips,
        small[:, :taps],
        small[:, taps],
        small[:, taps + 1],
        small[:, taps + 2],
        scatter(grad_in),
        scatter(jnp.sum(grad_ib, axis=0)),
        scatter(grad_out),
        small[:, taps + 3],
        small[:, taps + 4],
    )


def solution(mesh):
    both = ("dp", "fsdp")
    row, mat, cube = P(both), P(both, None), P(both, None, None)
    in_specs = (cube, mat, mat, row, row, row, mat, row, mat, row, row, cube)
    out_specs = (cube, cube, mat, row, row, row, mat, row, mat, row, row)
    return jax.shard_map(on_device, mesh=mesh, in_specs=in_specs, out_specs=out_specs, check_vma=False)
```

```python
from functools import partial
import jax
import jax.numpy as jnp
from jax import lax
from jax.experimental import pallas as pl
from jax.experimental.pallas import tpu as pltpu
from jax.sharding import PartitionSpec as P

F32 = jnp.float32
BF16 = jnp.bfloat16
PAD = 8
ROOT_HALF = 0.7071067811865476
LOG2E = 1.4426950408889634
INV_ROOT_2PI = 0.3989422804014327


def dot_nn(a, b):
    return lax.dot_general(a, b, (((1,), (0,)), ((), ())), preferred_element_type=F32)


def dot_nt(a, b):
    return lax.dot_general(a, b, (((1,), (1,)), ((), ())), preferred_element_type=F32)


def fold8(v):
    total = v[0:8]
    for r in range(8, v.shape[0], 8):
        total = total + v[r : r + 8]
    return total


def clip_kernel(
    live_ref,
    x_ref,
    dy_ref,
    w_in_ref,
    w_out_ref,
    rows_ref,
    ib_ref,
    out_ref,
    gx_ref,
    gin_ref,
    gout_ref,
    small_ref,
    gib_ref,
    xp,
    gm,
    xh,
    rs,
    nb,
    nbt,
    gob,
    gobt,
    ab,
    ghb,
    gn,
    acc_in,
    acc_out,
    acc_small,
    acc_ib,
    *,
    taps,
    hid_chunk,
    row_chunk,
):
    step = pl.program_id(0)
    frames, chans = xh.shape
    hid = ab.shape[1]
    margin = (taps - 1) // 2

    @pl.when(step == 0)
    def _():
        acc_in[...] = jnp.zeros_like(acc_in)
        acc_out[...] = jnp.zeros_like(acc_out)
        acc_small[...] = jnp.zeros_like(acc_small)
        acc_ib[...] = jnp.zeros_like(acc_ib)
        xp[0:PAD, :] = jnp.zeros((PAD, chans), F32)
        xp[PAD + frames :, :] = jnp.zeros((PAD, chans), F32)
        gm[0:PAD, :] = jnp.zeros((PAD, chans), F32)
        gm[PAD + frames :, :] = jnp.zeros((PAD, chans), F32)

    live = live_ref[step] != 0

    @pl.when(jnp.logical_not(live))
    def _():
        out_ref[...] = x_ref[...]
        gx_ref[...] = dy_ref[...]

    @pl.when(live)
    def _():
        def row(i):
            return rows_ref[i : i + 1, :]

        for r in range(0, frames, row_chunk):
            xp[PAD + r : PAD + r + row_chunk, :] = x_ref[0, r : r + row_chunk, :].astype(F32)
        for r in range(0, frames, row_chunk):
            base = PAD - margin + r
            mixed = row(taps) + xp[base : base + row_chunk, :] * row(0)
            for k in range(1, taps):
                mixed = mixed + xp[base + k : base + k + row_chunk, :] * row(k)
            center = mixed - jnp.mean(mixed, axis=-1, keepdims=True)
            var = jnp.mean(center * center, axis=-1, keepdims=True)
            inv = lax.rsqrt(var + 1e-06)
            xhat = center * inv
            xh[r : r + row_chunk, :] = xhat
            rs[r : r + row_chunk, :] = jnp.broadcast_to(inv, (row_chunk, 128))
            nb[r : r + row_chunk, :] = (xhat * row(taps + 1) + row(taps + 2)).astype(BF16)
            go = (dy_ref[0, r : r + row_chunk, :].astype(F32) * row(taps + 4)).astype(BF16)
            gob[r : r + row_chunk, :] = go
            acc_small[taps + 3, :, :] += fold8(go.astype(F32))
        nbt[...] = nb[...].T
        gobt[...] = gob[...].T

        for j in range(0, hid, hid_chunk):
            cols = slice(j, j + hid_chunk)
            h = dot_nn(nb[...], w_in_ref[:, cols]) + ib_ref[0:1, cols]
            u = h * ROOT_HALF
            cdf = 0.5 * lax.erf(u) + 0.5
            slope = cdf + h * (jnp.exp2(u * u * (-LOG2E)) * INV_ROOT_2PI)
            ab[:, cols] = (h * cdf).astype(BF16)
            ga = dot_nt(gob[...], w_out_ref[cols, :])
            gh = (ga * slope).astype(BF16)
            ghb[:, cols] = gh
            acc_ib[:, cols] += fold8(gh.astype(F32))
        gn[...] = dot_nt(ghb[...], w_in_ref[...])
        output = dot_nn(ab[...], w_out_ref[...]) + row(taps + 3)
        for r in range(0, frames, row_chunk):
            o = output[r : r + row_chunk, :]
            dy = dy_ref[0, r : r + row_chunk, :].astype(F32)
            acc_small[taps + 4, :, :] += fold8(dy * o)
            x = x_ref[0, r : r + row_chunk, :].astype(F32)
            out_ref[0, r : r + row_chunk, :] = (x + o * row(taps + 4)).astype(BF16)
        for j in range(0, hid, hid_chunk):
            cols = slice(j, j + hid_chunk)
            acc_out[:, cols] += dot_nn(gobt[...], ab[:, cols])
            acc_in[:, cols] += dot_nn(nbt[...], ghb[:, cols])

        for r in range(0, frames, row_chunk):
            g = gn[r : r + row_chunk, :]
            xhat = xh[r : r + row_chunk, :]
            gxh = g * xhat
            acc_small[taps + 2, :, :] += fold8(g)
            acc_small[taps + 1, :, :] += fold8(gxh)
            gg = g * row(taps + 1)
            m1 = jnp.mean(gg, axis=-1, keepdims=True)
            m2 = jnp.mean(gg * xhat, axis=-1, keepdims=True)
            gmix = rs[r : r + row_chunk, 0:1] * (gg - m1 - xhat * m2)
            acc_small[taps, :, :] += fold8(gmix)
            gm[PAD + r : PAD + r + row_chunk, :] = gmix
        for r in range(0, frames, row_chunk):
            base = PAD + margin + r
            x = xp[PAD + r : PAD + r + row_chunk, :]
            total = dy_ref[0, r : r + row_chunk, :].astype(F32)
            for k in range(taps):
                shifted = gm[base - k : base - k + row_chunk, :]
                total = total + shifted * row(k)
                acc_small[k, :, :] += fold8(shifted * x)
            gx_ref[0, r : r + row_chunk, :] = total.astype(BF16)

    @pl.when(step == pl.num_programs(0) - 1)
    def _():
        gin_ref[...] = acc_in[...].astype(gin_ref.dtype)
        for j in range(0, hid, 128):
            gout_ref[j : j + 128, :] = acc_out[:, j : j + 128].T.astype(gout_ref.dtype)
        small_ref[...] = acc_small[...]
        gib_ref[...] = acc_ib[...]


def clip_call(live, x, dy, w_in, w_out, rows, ib, taps, grad_dtype=F32):
    clips, frames, chans = x.shape
    hid = w_in.shape[1]
    clip_spec = pl.BlockSpec((1, frames, chans), lambda i, live: (i, 0, 0))
    whole = lambda shape: pl.BlockSpec(shape, lambda i, live: (0,) * len(shape), pipeline_mode=pl.Buffered(1))
    kinds = taps + 5
    return pl.pallas_call(
        partial(clip_kernel, taps=taps, hid_chunk=256, row_chunk=32),
        out_shape=(
            jax.ShapeDtypeStruct(x.shape, BF16),
            jax.ShapeDtypeStruct(x.shape, BF16),
            jax.ShapeDtypeStruct((chans, hid), grad_dtype),
            jax.ShapeDtypeStruct((hid, chans), grad_dtype),
            jax.ShapeDtypeStruct((kinds, 8, chans), F32),
            jax.ShapeDtypeStruct((8, hid), F32),
        ),
        grid_spec=pltpu.PrefetchScalarGridSpec(
            num_scalar_prefetch=1,
            grid=(clips,),
            in_specs=[
                clip_spec,
                clip_spec,
                whole((chans, hid)),
                whole((hid, chans)),
                whole(rows.shape),
                whole(ib.shape),
            ],
            out_specs=(
                clip_spec,
                clip_spec,
                whole((chans, hid)),
                whole((hid, chans)),
                whole((kinds, 8, chans)),
                whole((8, hid)),
            ),
            scratch_shapes=[
                pltpu.VMEM((frames + 2 * PAD, chans), F32),
                pltpu.VMEM((frames + 2 * PAD, chans), F32),
                pltpu.VMEM((frames, chans), F32),
                pltpu.VMEM((frames, 128), F32),
                pltpu.VMEM((frames, chans), BF16),
                pltpu.VMEM((chans, frames), BF16),
                pltpu.VMEM((frames, chans), BF16),
                pltpu.VMEM((chans, frames), BF16),
                pltpu.VMEM((frames, hid), BF16),
                pltpu.VMEM((frames, hid), BF16),
                pltpu.VMEM((frames, chans), F32),
                pltpu.VMEM((chans, hid), F32),
                pltpu.VMEM((chans, hid), F32),
                pltpu.VMEM((kinds, 8, chans), F32),
                pltpu.VMEM((8, hid), F32),
            ],
        ),
        compiler_params=pltpu.CompilerParams(vmem_limit_bytes=56 << 20),
        name="clips",
    )(live, x, dy, w_in, w_out, rows, ib)


MESH = pl.DeviceIdType.MESH


def grid_of(mesh_shape):
    across = mesh_shape["dp"] // 2
    deep = mesh_shape["fsdp"]
    tall = across if deep % across == 0 else 1
    return across, tall, deep // tall


def place(sizes):
    dp = lax.axis_index("dp")
    fsdp = lax.axis_index("fsdp")
    return dp // 2, dp % 2, fsdp // sizes[1], fsdp % sizes[1]


def at(sizes, x, core, z, y):
    return {"dp": x * 2 + core, "fsdp": z * sizes[1] + y}


def partners(sizes):
    x, core, z, y = place(sizes)
    across, tall, deep = sizes
    found = [at(sizes, x, 1 - core, z, y)]
    found += [at(sizes, (x + o) % across, core, z, y) for o in range(1, across)]
    found += [at(sizes, x, core, z, (y + o) % tall) for o in range(1, tall)]
    found += [at(sizes, x, core, (z + o) % deep, y) for o in range(1, deep)]
    return found


def greet(sizes):
    barrier = pltpu.get_barrier_semaphore()
    others = partners(sizes)
    for other in others:
        pl.semaphore_signal(barrier, inc=1, device_id=other, device_id_type=MESH)
    pl.semaphore_wait(barrier, len(others))


def send(src, dst, send_sems, recv_sems, slot, device):
    copy = pltpu.make_async_remote_copy(
        src_ref=src,
        dst_ref=dst,
        send_sem=send_sems.at[slot],
        recv_sem=recv_sems.at[slot],
        device_id=device,
        device_id_type=MESH,
    )
    copy.start()
    return copy


class Slots:
    def __init__(self):
        self.used = 0

    def take(self):
        self.used += 1
        return self.used - 1


def gather_copies(sizes):
    across, tall, deep = sizes
    columns = across * tall
    return 3 * ((deep - 1) + (columns - 1) + columns)


def gather_kernel(small_ref, in_ref, out_ref, full_small, full_in, full_out, send_sems, recv_sems, local_sems, *, sizes):
    across, tall, deep = sizes
    x, core, z, y = place(sizes)
    slots = Slots()
    greet(sizes)
    own = (small_ref, in_ref, out_ref)
    full = (full_small, full_in, full_out)
    x_first = (True, True, False)

    lines = []
    keeps = []
    for i in range(3):
        keep = pltpu.make_async_copy(own[i], full[i].at[x, core, z, y], local_sems.at[i])
        keep.start()
        keeps.append(keep)
        line = []
        for o in range(1, deep):
            line.append(
                send(own[i], full[i].at[x, core, z, y], send_sems, recv_sems, slots.take(), at(sizes, x, core, (z + o) % deep, y))
            )
        lines.append(line)
    started = [c for line in lines for c in line]

    def column(i, cx, cy):
        return full[i].at[cx, core, :, cy]

    def move(i, cx, cy, device):
        copy = send(column(i, cx, cy), column(i, cx, cy), send_sems, recv_sems, slots.take(), device)
        started.append(copy)
        return copy

    firsts, seconds, sides = [], [], []
    for i in range(3):
        keeps[i].wait()
        for copy in lines[i]:
            copy.wait_recv()
        along_x = [move(i, x, y, at(sizes, (x + o) % across, core, z, y)) for o in range(1, across)]
        along_y = [move(i, x, y, at(sizes, x, core, z, (y + o) % tall)) for o in range(1, tall)]
        firsts.append((along_x, along_y))
        sides.append(move(i, x, y, at(sizes, x, 1 - core, z, y)))
    for i in range(3):
        along_x, along_y = firsts[i]
        passed = []
        if x_first[i]:
            for o, copy in zip(range(1, across), along_x):
                copy.wait_recv()
                cx = (x - o + across) % across
                passed.append([move(i, cx, y, at(sizes, x, core, z, (y + p) % tall)) for p in range(1, tall)])
                sides.append(move(i, cx, y, at(sizes, x, 1 - core, z, y)))
            for o, copy in zip(range(1, tall), along_y):
                copy.wait_recv()
                sides.append(move(i, x, (y - o + tall) % tall, at(sizes, x, 1 - core, z, y)))
        else:
            for o, copy in zip(range(1, tall), along_y):
                copy.wait_recv()
                cy = (y - o + tall) % tall
                passed.append([move(i, x, cy, at(sizes, (x + p) % across, core, z, y)) for p in range(1, across)])
                sides.append(move(i, x, cy, at(sizes, x, 1 - core, z, y)))
            for o, copy in zip(range(1, across), along_x):
                copy.wait_recv()
                sides.append(move(i, (x - o + across) % across, y, at(sizes, x, 1 - core, z, y)))
        seconds.append(passed)
    for i in range(3):
        for o, row in enumerate(seconds[i], 1):
            for p, copy in enumerate(row, 1):
                copy.wait_recv()
                if x_first[i]:
                    cx, cy = (x - o + across) % across, (y - p + tall) % tall
                else:
                    cx, cy = (x - p + across) % across, (y - o + tall) % tall
                sides.append(move(i, cx, cy, at(sizes, x, 1 - core, z, y)))
    for copy in sides:
        copy.wait_recv()
    for copy in started:
        copy.wait_send()


def gather_call(sizes, small, w_in, w_out):
    across, tall, deep = sizes
    copies = gather_copies(sizes)
    shards = (small, w_in, w_out)
    vmem = pl.BlockSpec(memory_space=pltpu.VMEM)
    return pl.pallas_call(
        partial(gather_kernel, sizes=sizes),
        out_shape=tuple(jax.ShapeDtypeStruct((across, 2, deep, tall) + s.shape, s.dtype) for s in shards),
        in_specs=[vmem] * 3,
        out_specs=(pl.BlockSpec(memory_space=pl.ANY),) * 3,
        scratch_shapes=[
            pltpu.SemaphoreType.DMA((copies,)),
            pltpu.SemaphoreType.DMA((copies,)),
            pltpu.SemaphoreType.DMA((3,)),
        ],
        compiler_params=pltpu.CompilerParams(collective_id=0, has_side_effects=True),
        name="gather",
    )(*shards)


def scatter_copies(sizes):
    across, tall, deep = sizes
    columns = across * tall
    return 3 * (columns + (columns - 1) + (deep - 1))


def add_into(dst, terms):
    def block(k, carry):
        total = terms[0][k].astype(F32)
        for term in terms[1:]:
            total = total + term[k].astype(F32)
        dst[k] = total.astype(dst.dtype)
        return carry

    lax.fori_loop(0, dst.shape[0], block, 0)


def scatter_kernel(*refs, sizes):
    across, tall, deep = sizes
    parts = refs[0:3]
    outs = refs[3:6]
    side = refs[6:9]
    held = refs[9:12]
    corner = refs[12:15]
    mixed = refs[15:18]
    direct = refs[18:21]
    routed = refs[21:24]
    total = refs[24:27]
    lines = refs[27:30]
    send_sems, recv_sems = refs[30:32]
    x, core, z, y = place(sizes)
    slots = Slots()
    greet(sizes)
    x_first = (True, True, False)
    started = []

    def move(src, dst, device):
        copy = send(src, dst, send_sems, recv_sems, slots.take(), device)
        started.append(copy)
        return copy

    def far(i, a, b):
        if x_first[i]:
            return (x + a) % across, (y + b) % tall
        return (x + b) % across, (y + a) % tall

    def lengths(i):
        return (across, tall) if x_first[i] else (tall, across)

    def peer(i, a, b):
        cx, cy = far(i, a, b)
        return at(sizes, cx, core, z, cy)

    order = {}
    for i in range(3):
        last, first = lengths(i)
        order[i] = [(a, b) for a in range(1, last) for b in range(1, first)]
        order[i] += [(0, b) for b in range(1, first)]
        order[i] += [(a, 0) for a in range(1, last)] + [(0, 0)]
    crossings = {}
    for k in range(across * tall):
        for i in range(3):
            cx, cy = far(i, *order[i][k])
            crossings[i, order[i][k]] = move(
                parts[i].at[cx, 1 - core, :, cy], side[i].at[cx, cy], at(sizes, x, 1 - core, z, y)
            )

    def own(i, a, b):
        cx, cy = far(i, a, b)
        crossings[i, (a, b)].wait_recv()
        add_into(held[i].at[cx, cy], [parts[i].at[cx, core, :, cy], side[i].at[cx, cy]])
        return held[i].at[cx, cy]

    corners, directs, routeds = {}, {}, {}
    for i in range(3):
        last, first = lengths(i)
        for a in range(1, last):
            for b in range(1, first):
                src = own(i, a, b)
                corners[i, a, b] = move(src, corner[i].at[a - 1, b - 1], peer(i, 0, b))
    for i in range(3):
        last, first = lengths(i)
        for b in range(1, first):
            src = own(i, 0, b)
            directs[i, b] = move(src, direct[i].at[b - 1], peer(i, 0, b))
    for i in range(3):
        last, first = lengths(i)
        for a in range(1, last):
            src = own(i, a, 0)
            terms = [src]
            for b in range(1, first):
                corners[i, a, b].wait_recv()
                terms.append(corner[i].at[a - 1, b - 1])
            add_into(mixed[i].at[a - 1], terms)
            routeds[i, a] = move(mixed[i].at[a - 1], routed[i].at[a - 1], peer(i, a, 0))
    ends = {}
    for i in range(3):
        last, first = lengths(i)
        terms = [own(i, 0, 0)]
        for b in range(1, first):
            directs[i, b].wait_recv()
            terms.append(direct[i].at[b - 1])
        for a in range(1, last):
            routeds[i, a].wait_recv()
            terms.append(routed[i].at[a - 1])
        add_into(total[i], terms)
        for o in range(1, deep):
            ends[i, o] = move(
                total[i].at[(z + o) % deep], lines[i].at[o - 1], at(sizes, x, core, (z + o) % deep, y)
            )
    for i in range(3):
        value = total[i][z].astype(F32)
        for o in range(1, deep):
            ends[i, o].wait_recv()
            value = value + lines[i][o - 1].astype(F32)
        outs[i][...] = value
    for copy in started:
        copy.wait_send()


def scatter_call(sizes, small, g_in, g_out):
    across, tall, deep = sizes
    copies = scatter_copies(sizes)
    parts = (small, g_in, g_out)
    vmem = pl.BlockSpec(memory_space=pltpu.VMEM)
    pieces = [p.shape[4:] for p in parts]
    kinds = [p.dtype for p in parts]

    def scratch(lead):
        return [pltpu.VMEM(lead(i) + pieces[i], kinds[i]) for i in range(3)]

    last = (across, across, tall)
    first = (tall, tall, across)
    grid = lambda i: (across, tall, deep)
    return pl.pallas_call(
        partial(scatter_kernel, sizes=sizes),
        out_shape=tuple(jax.ShapeDtypeStruct(p, F32) for p in pieces),
        in_specs=[vmem] * 3,
        out_specs=(vmem,) * 3,
        scratch_shapes=[
            *scratch(grid),
            *scratch(grid),
            *scratch(lambda i: (max(last[i] - 1, 1), max(first[i] - 1, 1), deep)),
            *scratch(lambda i: (max(last[i] - 1, 1), deep)),
            *scratch(lambda i: (max(first[i] - 1, 1), deep)),
            *scratch(lambda i: (max(last[i] - 1, 1), deep)),
            *scratch(lambda i: (deep,)),
            *scratch(lambda i: (max(deep - 1, 1),)),
            pltpu.SemaphoreType.DMA((copies,)),
            pltpu.SemaphoreType.DMA((copies,)),
        ],
        compiler_params=pltpu.CompilerParams(collective_id=1, has_side_effects=True, vmem_limit_bytes=60 << 20),
        name="scatter",
    )(*parts)


def on_device(
    mel_clips,
    live_counts,
    conv_weight,
    conv_bias,
    norm_gain,
    norm_shift,
    in_weight,
    in_bias,
    out_weight,
    out_bias,
    layer_scale,
    cotangent,
    *,
    sizes,
):
    taps = conv_weight.shape[1]
    kinds = taps + 5
    micro_count = live_counts.shape[1]
    slot_count = mel_clips.shape[0] // micro_count
    shard, hid = in_weight.shape
    devices = lax.axis_size(("dp", "fsdp"))
    chans = shard * devices
    ratio = in_bias.shape[0] // shard
    spare = 128 - kinds - ratio

    columns = jnp.stack([conv_bias, norm_gain, norm_shift, out_bias, layer_scale], axis=1)
    small = jnp.concatenate([conv_weight, columns, in_bias.reshape(shard, ratio)], axis=1)
    small = jnp.pad(small, ((0, 0), (0, spare)))
    small, full_in, full_out = gather_call(sizes, small, in_weight, out_weight)
    small = small.reshape(chans, 128)
    rows = jnp.pad(small[:, :kinds].T.astype(F32), ((0, 16 - kinds), (0, 0)))
    bias_row = small[:, kinds : kinds + ratio].reshape(1, hid).astype(F32)
    bias_row = jnp.broadcast_to(bias_row, (8, hid))
    live = (lax.iota(jnp.int32, slot_count)[None, :] < live_counts[0][:, None]).astype(jnp.int32)

    block_out, grad_clips, grad_in, grad_out, small, grad_ib = clip_call(
        live.reshape(-1),
        mel_clips,
        cotangent,
        full_in.reshape(chans, hid),
        full_out.reshape(hid, chans),
        rows,
        bias_row,
        taps,
        BF16,
    )
    lead = (sizes[0], 2, sizes[2], sizes[1])
    small = jnp.sum(small, axis=1).T
    grad_ib = jnp.sum(grad_ib, axis=0).reshape(chans, ratio)
    small = jnp.pad(jnp.concatenate([small, grad_ib], axis=1), ((0, 0), (0, spare)))
    small, grad_in, grad_out = scatter_call(
        sizes,
        small.reshape(lead + (shard, 128)),
        grad_in.reshape(lead + in_weight.shape),
        grad_out.reshape(lead + out_weight.shape),
    )
    return (
        block_out,
        grad_clips,
        small[:, :taps],
        small[:, taps],
        small[:, taps + 1],
        small[:, taps + 2],
        grad_in,
        small[:, kinds : kinds + ratio].reshape(-1),
        grad_out,
        small[:, taps + 3],
        small[:, taps + 4],
    )


def solution(mesh):
    both = ("dp", "fsdp")
    row, mat, cube = P(both), P(both, None), P(both, None, None)
    in_specs = (cube, mat, mat, row, row, row, mat, row, mat, row, row, cube)
    out_specs = (cube, cube, mat, row, row, row, mat, row, mat, row, row)
    body = partial(on_device, sizes=grid_of(mesh.shape))
    return jax.shard_map(body, mesh=mesh, in_specs=in_specs, out_specs=out_specs, check_vma=False)
```

```python
from functools import partial
import jax
import jax.numpy as jnp
from jax import lax
from jax.experimental import pallas as pl
from jax.experimental.pallas import tpu as pltpu
from jax.sharding import PartitionSpec as P

F32 = jnp.float32
BF16 = jnp.bfloat16
PAD = 8
ROOT_HALF = 0.7071067811865476
LOG2E = 1.4426950408889634
INV_ROOT_2PI = 0.3989422804014327


def dot_nn(a, b):
    return lax.dot_general(a, b, (((1,), (0,)), ((), ())), preferred_element_type=F32)


def dot_nt(a, b):
    return lax.dot_general(a, b, (((1,), (1,)), ((), ())), preferred_element_type=F32)


def fold8(v):
    total = v[0:8]
    for r in range(8, v.shape[0], 8):
        total = total + v[r : r + 8]
    return total


def clip_of(i, counts, slots):
    micros = counts.shape[0]
    lives = [counts[m] for m in range(micros)]
    count = lives[0]
    for m in range(1, micros):
        count = count + lives[m]
    alive = i < count
    rest = jnp.where(alive, i, i - count)
    clip = jnp.int32(0)
    start = jnp.int32(0)
    for m in range(micros):
        length = jnp.where(alive, lives[m], slots - lives[m])
        inside = jnp.logical_and(rest >= start, rest < start + length)
        first = m * slots + jnp.where(alive, 0, lives[m])
        clip = jnp.where(inside, first + rest - start, clip)
        start = start + length
    return clip


def lane_ids(rows):
    return lax.broadcasted_iota(jnp.int32, (rows, 128), 1)


def unpack_small(pieces_ref, kinds, rows_ref, ib_ref):
    devices = pieces_ref.shape[0]
    shard = rows_ref.shape[1] // devices
    wide = ib_ref.shape[1] // devices
    rows_ref[...] = jnp.zeros_like(rows_ref)
    ib_ref[...] = jnp.zeros_like(ib_ref)
    lane = lane_ids(8)
    for d in range(devices):
        piece = pieces_ref[d].astype(F32)
        at, off = divmod(d * shard, 128)
        rows_ref[:, at * 128 : at * 128 + 128] += pltpu.roll(piece, off, 1)
        at, off = divmod(d * wide, 128)
        moved = pltpu.roll(piece[8:16], off, 1)[kinds - 8 : kinds - 7]
        line = lane[0:1]
        ib_ref[0:1, at * 128 : at * 128 + 128] += jnp.where(line >= off, moved, 0.0)
        if off + wide > 128:
            ib_ref[0:1, at * 128 + 128 : at * 128 + 256] += jnp.where(line < off, moved, 0.0)


def pack_small(acc_small, acc_ib, rows_ref, small_ref):
    devices = small_ref.shape[0]
    kinds = acc_small.shape[0]
    shard = rows_ref.shape[1] // devices
    wide = acc_ib.shape[1] // devices
    for k in range(kinds):
        rows_ref[k : k + 1, :] = jnp.sum(acc_small[k], axis=0, keepdims=True)
    lane = lane_ids(16)
    bias = acc_ib[...]
    for d in range(devices):
        at, off = divmod(d * shard, 128)
        moved = pltpu.roll(rows_ref[:, at * 128 : at * 128 + 128], (128 - off) % 128, 1)
        small_ref[d] = jnp.where(lane < shard, moved, 0.0)
        at, off = divmod(d * wide, 128)
        moved = pltpu.roll(bias[:, at * 128 : at * 128 + 128], (128 - off) % 128, 1)
        if off + wide > 128:
            later = pltpu.roll(bias[:, at * 128 + 128 : at * 128 + 256], 128 - off, 1)
            moved = jnp.where(lane[0:8] < 128 - off, moved, later)
        moved = jnp.where(lane[0:8] < wide, moved, 0.0)
        small_ref[d, kinds : kinds + 1, :] = jnp.sum(moved, axis=0, keepdims=True)


def clip_kernel(
    counts_ref,
    x_ref,
    dy_ref,
    xn_ref,
    dyn_ref,
    w_in_ref,
    w_out_ref,
    pieces_ref,
    out_ref,
    gx_ref,
    gin_ref,
    gout_ref,
    small_ref,
    rows_ref,
    ib_ref,
    xp,
    gm,
    xh,
    rs,
    left,
    acts,
    gob,
    nb,
    gn,
    raw,
    acc,
    acc_small,
    acc_ib,
    *,
    taps,
    hid_chunk,
    row_chunk,
    parts,
):
    step = pl.program_id(0)
    _, groups, frames, lanes = xh.shape
    chans = groups * lanes
    hid = acts.shape[2]
    margin = (taps - 1) // 2
    gain, shift, obias, scale = taps + 1, taps + 2, taps + 3, taps + 4
    span = [slice(g * lanes, (g + 1) * lanes) for g in range(groups)]
    now = step % 2
    then = 1 - now
    live_count = counts_ref[0]
    for m in range(1, counts_ref.shape[0]):
        live_count = live_count + counts_ref[m]
    live = step < live_count

    def row(i, g):
        return rows_ref[i : i + 1, span[g]]

    def total(blocks):
        added = blocks[0]
        for block in blocks[1:]:
            added = added + block
        return jnp.sum(added, axis=-1, keepdims=True) * (1.0 / chans)

    def stage(x_in, to):
        for g in range(groups):
            xp[to, g, PAD : PAD + frames, :] = x_in[0, :, span[g]].astype(F32)

    def begin(dy_in, to, start, size):
        for r in range(0, size, row_chunk):
            low = start + r
            at_rows = pl.ds(low, row_chunk)
            mixed = []
            for g in range(groups):
                m = row(taps, g) + xp[to, g, pl.ds(low + (PAD - margin), row_chunk), :] * row(0, g)
                for k in range(1, taps):
                    m = m + xp[to, g, pl.ds(low + (PAD - margin + k), row_chunk), :] * row(k, g)
                mixed.append(m)
            mean = total(mixed)
            center = [m - mean for m in mixed]
            inv = lax.rsqrt(total([c * c for c in center]) + 1e-06)
            rs[to, at_rows, :] = jnp.broadcast_to(inv, (row_chunk, lanes))
            for g in range(groups):
                xhat = center[g] * inv
                xh[to, g, at_rows, :] = xhat
                nb[to, at_rows, span[g]] = (xhat * row(gain, g) + row(shift, g)).astype(BF16)
                gob[to, at_rows, span[g]] = (dy_in[0, at_rows, span[g]].astype(F32) * row(scale, g)).astype(BF16)

    def turn(to):
        left[to, 0] = gob[to].T
        left[to, 1] = nb[to].T

    @pl.when(step == 0)
    def _():
        unpack_small(pieces_ref, taps + 5, rows_ref, ib_ref)
        acc[...] = jnp.zeros_like(acc)
        acc_small[...] = jnp.zeros_like(acc_small)
        acc_ib[...] = jnp.zeros_like(acc_ib)
        edge = jnp.zeros((2, groups, PAD, lanes), F32)
        xp[:, :, 0:PAD, :] = edge
        xp[:, :, PAD + frames :, :] = edge
        gm[:, 0:PAD, :] = edge[0]
        gm[:, PAD + frames :, :] = edge[0]
        stage(x_ref, 0)
        begin(dy_ref, 0, 0, frames)
        turn(0)

    @pl.when(jnp.logical_not(live))
    def _():
        out_ref[...] = x_ref[...]
        gx_ref[...] = dy_ref[...]

    @pl.when(live)
    def _():
        stage(xn_ref, then)
        for j in range(0, hid, hid_chunk):
            cols = slice(j, j + hid_chunk)
            h = dot_nn(nb[now], w_in_ref[:, cols]) + ib_ref[0:1, cols]
            u = h * ROOT_HALF
            cdf = 0.5 * lax.erf(u) + 0.5
            slope = cdf + h * (jnp.exp2(u * u * (-LOG2E)) * INV_ROOT_2PI)
            acts[0, :, cols] = (h * cdf).astype(BF16)
            ga = dot_nt(gob[now], w_out_ref[cols, :])
            gh = (ga * slope).astype(BF16)
            acts[1, :, cols] = gh
            acc_ib[:, cols] += fold8(gh.astype(F32))

        wide = 256
        tall = frames // (2 * (chans // wide))
        for c in range(0, chans, wide):
            spot = 2 * (c // wide) * tall
            gn[:, c : c + wide] = dot_nt(acts[1], w_in_ref[c : c + wide, :])
            begin(dyn_ref, then, spot, tall)
            raw[:, c : c + wide] = dot_nn(acts[0], w_out_ref[:, c : c + wide])
            begin(dyn_ref, then, spot + tall, tall)
        turn(then)

        rows_each = frames // parts
        units = 2 * (hid // hid_chunk)

        def norm_back(base):
            at_rows = pl.ds(base, rows_each)
            hats = [xh[now, g, at_rows, :] for g in range(groups)]
            grads = [gn[at_rows, span[g]] for g in range(groups)]
            gained = []
            for g in range(groups):
                acc_small[shift, :, span[g]] += fold8(grads[g])
                acc_small[gain, :, span[g]] += fold8(grads[g] * hats[g])
                gained.append(grads[g] * row(gain, g))
            mean = total(gained)
            slant = total([v * h for v, h in zip(gained, hats)])
            inv = rs[now, at_rows, :]
            for g in range(groups):
                gmix = inv * (gained[g] - mean - hats[g] * slant)
                acc_small[taps, :, span[g]] += fold8(gmix)
                gm[g, pl.ds(base + PAD, rows_each), :] = gmix

        def finish(base):
            at_rows = pl.ds(base, rows_each)
            for g in range(groups):
                o = raw[at_rows, span[g]] + row(obias, g)
                dy = dy_ref[0, at_rows, span[g]].astype(F32)
                acc_small[scale, :, span[g]] += fold8(dy * o)
                acc_small[obias, :, span[g]] += fold8(gob[now, at_rows, span[g]].astype(F32))
                x = xp[now, g, pl.ds(base + PAD, rows_each), :]
                out_ref[0, at_rows, span[g]] = (x + o * row(scale, g)).astype(BF16)

        def conv_back(base):
            at_rows = pl.ds(base, rows_each)
            for g in range(groups):
                x = xp[now, g, pl.ds(base + PAD, rows_each), :]
                grad = dy_ref[0, at_rows, span[g]].astype(F32)
                for k in range(taps):
                    moved = gm[g, pl.ds(base + (PAD + margin - k), rows_each), :]
                    grad = grad + moved * row(k, g)
                    acc_small[k, :, span[g]] += fold8(moved * x)
                gx_ref[0, at_rows, span[g]] = grad.astype(BF16)

        def weights(unit):
            side, place = unit % 2, unit // 2
            cols = slice(place * hid_chunk, (place + 1) * hid_chunk)
            acc[side, :, cols] += dot_nn(left[now, side], acts[side, :, cols])

        done = 0
        for i in range(parts):
            upto = units * (i + 1) // parts
            norm_back(i * rows_each)
            for unit in range(done, upto):
                weights(unit)
            done = upto
            finish(i * rows_each)
            if i > 0:
                conv_back((i - 1) * rows_each)
        conv_back(frames - rows_each)

    @pl.when(step == pl.num_programs(0) - 1)
    def _():
        gin_ref[...] = acc[1].astype(gin_ref.dtype)
        for j in range(0, hid, 128):
            gout_ref[j : j + 128, :] = acc[0, :, j : j + 128].T.astype(gout_ref.dtype)
        pack_small(acc_small, acc_ib, rows_ref, small_ref)


def clip_call(counts, x, dy, w_in, w_out, pieces, taps, grad_dtype=BF16):
    clips, frames, chans = x.shape
    hid = w_in.shape[1]
    slots = clips // counts.shape[0]
    kinds = taps + 5

    def clip_spec(ahead):
        def index(i, counts):
            return clip_of(jnp.minimum(i + ahead, clips - 1), counts, slots), 0, 0

        return pl.BlockSpec((1, frames, chans), index)

    def whole(shape):
        return pl.BlockSpec(shape, lambda i, counts: (0,) * len(shape), pipeline_mode=pl.Buffered(1))

    groups = chans // 128
    return pl.pallas_call(
        partial(clip_kernel, taps=taps, hid_chunk=256, row_chunk=32, parts=8),
        out_shape=(
            jax.ShapeDtypeStruct(x.shape, BF16),
            jax.ShapeDtypeStruct(x.shape, BF16),
            jax.ShapeDtypeStruct((chans, hid), grad_dtype),
            jax.ShapeDtypeStruct((hid, chans), grad_dtype),
            jax.ShapeDtypeStruct(pieces.shape, F32),
        ),
        grid_spec=pltpu.PrefetchScalarGridSpec(
            num_scalar_prefetch=1,
            grid=(clips,),
            in_specs=[
                clip_spec(0),
                clip_spec(0),
                clip_spec(1),
                clip_spec(1),
                whole((chans, hid)),
                whole((hid, chans)),
                whole(pieces.shape),
            ],
            out_specs=(
                clip_spec(0),
                clip_spec(0),
                whole((chans, hid)),
                whole((hid, chans)),
                whole(pieces.shape),
            ),
            scratch_shapes=[
                pltpu.VMEM((16, chans), F32),
                pltpu.VMEM((8, hid), F32),
                pltpu.VMEM((2, groups, frames + 2 * PAD, 128), F32),
                pltpu.VMEM((groups, frames + 2 * PAD, 128), F32),
                pltpu.VMEM((2, groups, frames, 128), F32),
                pltpu.VMEM((2, frames, 128), F32),
                pltpu.VMEM((2, 2, chans, frames), BF16),
                pltpu.VMEM((2, frames, hid), BF16),
                pltpu.VMEM((2, frames, chans), BF16),
                pltpu.VMEM((2, frames, chans), BF16),
                pltpu.VMEM((frames, chans), F32),
                pltpu.VMEM((frames, chans), F32),
                pltpu.VMEM((2, chans, hid), F32),
                pltpu.VMEM((kinds, 8, chans), F32),
                pltpu.VMEM((8, hid), F32),
            ],
        ),
        compiler_params=pltpu.CompilerParams(vmem_limit_bytes=60 << 20),
        name="clips",
    )(counts, x, dy, x, dy, w_in, w_out, pieces)


MESH = pl.DeviceIdType.MESH


def grid_of(mesh_shape):
    across = mesh_shape["dp"] // 2
    deep = mesh_shape["fsdp"]
    tall = across if deep % across == 0 else 1
    return across, tall, deep // tall


def place(sizes):
    dp = lax.axis_index("dp")
    fsdp = lax.axis_index("fsdp")
    return dp // 2, dp % 2, fsdp // sizes[1], fsdp % sizes[1]


def at(sizes, x, core, z, y):
    return {"dp": x * 2 + core, "fsdp": z * sizes[1] + y}


def partners(sizes):
    x, core, z, y = place(sizes)
    across, tall, deep = sizes
    found = [at(sizes, x, 1 - core, z, y)]
    found += [at(sizes, (x + o) % across, core, z, y) for o in range(1, across)]
    found += [at(sizes, x, core, z, (y + o) % tall) for o in range(1, tall)]
    found += [at(sizes, x, core, (z + o) % deep, y) for o in range(1, deep)]
    return found


def greet(sizes):
    barrier = pltpu.get_barrier_semaphore()
    others = partners(sizes)
    for other in others:
        pl.semaphore_signal(barrier, inc=1, device_id=other, device_id_type=MESH)
    pl.semaphore_wait(barrier, len(others))


def send(src, dst, send_sems, recv_sems, slot, device):
    copy = pltpu.make_async_remote_copy(
        src_ref=src,
        dst_ref=dst,
        send_sem=send_sems.at[slot],
        recv_sem=recv_sems.at[slot],
        device_id=device,
        device_id_type=MESH,
    )
    copy.start()
    return copy


class Slots:
    def __init__(self):
        self.used = 0

    def take(self):
        self.used += 1
        return self.used - 1


def gather_copies(sizes):
    across, tall, deep = sizes
    columns = across * tall
    return 3 * ((deep - 1) + (columns - 1) + columns)


def gather_kernel(small_ref, in_ref, out_ref, full_small, full_in, full_out, send_sems, recv_sems, local_sems, *, sizes):
    across, tall, deep = sizes
    x, core, z, y = place(sizes)
    slots = Slots()
    greet(sizes)
    own = (small_ref, in_ref, out_ref)
    full = (full_small, full_in, full_out)
    x_first = (True, True, False)

    lines = []
    keeps = []
    for i in range(3):
        keep = pltpu.make_async_copy(own[i], full[i].at[x, core, z, y], local_sems.at[i])
        keep.start()
        keeps.append(keep)
        line = []
        for o in range(1, deep):
            line.append(
                send(own[i], full[i].at[x, core, z, y], send_sems, recv_sems, slots.take(), at(sizes, x, core, (z + o) % deep, y))
            )
        lines.append(line)
    started = [c for line in lines for c in line]

    def column(i, cx, cy):
        return full[i].at[cx, core, :, cy]

    def move(i, cx, cy, device):
        copy = send(column(i, cx, cy), column(i, cx, cy), send_sems, recv_sems, slots.take(), device)
        started.append(copy)
        return copy

    firsts, seconds, sides = [], [], []
    for i in range(3):
        keeps[i].wait()
        for copy in lines[i]:
            copy.wait_recv()
        along_x = [move(i, x, y, at(sizes, (x + o) % across, core, z, y)) for o in range(1, across)]
        along_y = [move(i, x, y, at(sizes, x, core, z, (y + o) % tall)) for o in range(1, tall)]
        firsts.append((along_x, along_y))
        sides.append(move(i, x, y, at(sizes, x, 1 - core, z, y)))
    for i in range(3):
        along_x, along_y = firsts[i]
        passed = []
        if x_first[i]:
            for o, copy in zip(range(1, across), along_x):
                copy.wait_recv()
                cx = (x - o + across) % across
                passed.append([move(i, cx, y, at(sizes, x, core, z, (y + p) % tall)) for p in range(1, tall)])
                sides.append(move(i, cx, y, at(sizes, x, 1 - core, z, y)))
            for o, copy in zip(range(1, tall), along_y):
                copy.wait_recv()
                sides.append(move(i, x, (y - o + tall) % tall, at(sizes, x, 1 - core, z, y)))
        else:
            for o, copy in zip(range(1, tall), along_y):
                copy.wait_recv()
                cy = (y - o + tall) % tall
                passed.append([move(i, x, cy, at(sizes, (x + p) % across, core, z, y)) for p in range(1, across)])
                sides.append(move(i, x, cy, at(sizes, x, 1 - core, z, y)))
            for o, copy in zip(range(1, across), along_x):
                copy.wait_recv()
                sides.append(move(i, (x - o + across) % across, y, at(sizes, x, 1 - core, z, y)))
        seconds.append(passed)
    for i in range(3):
        for o, row in enumerate(seconds[i], 1):
            for p, copy in enumerate(row, 1):
                copy.wait_recv()
                if x_first[i]:
                    cx, cy = (x - o + across) % across, (y - p + tall) % tall
                else:
                    cx, cy = (x - p + across) % across, (y - o + tall) % tall
                sides.append(move(i, cx, cy, at(sizes, x, 1 - core, z, y)))
    for copy in sides:
        copy.wait_recv()
    for copy in started:
        copy.wait_send()


def gather_call(sizes, small, w_in, w_out):
    across, tall, deep = sizes
    copies = gather_copies(sizes)
    shards = (small, w_in, w_out)
    vmem = pl.BlockSpec(memory_space=pltpu.VMEM)
    return pl.pallas_call(
        partial(gather_kernel, sizes=sizes),
        out_shape=tuple(jax.ShapeDtypeStruct((across, 2, deep, tall) + s.shape, s.dtype) for s in shards),
        in_specs=[vmem] * 3,
        out_specs=(pl.BlockSpec(memory_space=pl.ANY),) * 3,
        scratch_shapes=[
            pltpu.SemaphoreType.DMA((copies,)),
            pltpu.SemaphoreType.DMA((copies,)),
            pltpu.SemaphoreType.DMA((3,)),
        ],
        compiler_params=pltpu.CompilerParams(collective_id=0, has_side_effects=True),
        name="gather",
    )(*shards)


def scatter_copies(sizes):
    across, tall, deep = sizes
    columns = across * tall
    return 3 * (columns + (columns - 1) + (deep - 1))


def add_into(dst, terms):
    def block(k, carry):
        total = terms[0][k].astype(F32)
        for term in terms[1:]:
            total = total + term[k].astype(F32)
        dst[k] = total.astype(dst.dtype)
        return carry

    lax.fori_loop(0, dst.shape[0], block, 0)


def scatter_kernel(*refs, sizes):
    across, tall, deep = sizes
    parts = refs[0:3]
    outs = refs[3:6]
    side = refs[6:9]
    held = refs[9:12]
    corner = refs[12:15]
    mixed = refs[15:18]
    direct = refs[18:21]
    routed = refs[21:24]
    total = refs[24:27]
    lines = refs[27:30]
    send_sems, recv_sems = refs[30:32]
    x, core, z, y = place(sizes)
    slots = Slots()
    greet(sizes)
    x_first = (True, True, False)
    started = []

    def move(src, dst, device):
        copy = send(src, dst, send_sems, recv_sems, slots.take(), device)
        started.append(copy)
        return copy

    def far(i, a, b):
        if x_first[i]:
            return (x + a) % across, (y + b) % tall
        return (x + b) % across, (y + a) % tall

    def lengths(i):
        return (across, tall) if x_first[i] else (tall, across)

    def peer(i, a, b):
        cx, cy = far(i, a, b)
        return at(sizes, cx, core, z, cy)

    order = {}
    for i in range(3):
        last, first = lengths(i)
        order[i] = [(a, b) for a in range(1, last) for b in range(1, first)]
        order[i] += [(0, b) for b in range(1, first)]
        order[i] += [(a, 0) for a in range(1, last)] + [(0, 0)]
    crossings = {}
    for k in range(across * tall):
        for i in range(3):
            cx, cy = far(i, *order[i][k])
            crossings[i, order[i][k]] = move(
                parts[i].at[cx, 1 - core, :, cy], side[i].at[cx, cy], at(sizes, x, 1 - core, z, y)
            )

    def own(i, a, b):
        cx, cy = far(i, a, b)
        crossings[i, (a, b)].wait_recv()
        add_into(held[i].at[cx, cy], [parts[i].at[cx, core, :, cy], side[i].at[cx, cy]])
        return held[i].at[cx, cy]

    corners, directs, routeds = {}, {}, {}
    for i in range(3):
        last, first = lengths(i)
        for a in range(1, last):
            for b in range(1, first):
                src = own(i, a, b)
                corners[i, a, b] = move(src, corner[i].at[a - 1, b - 1], peer(i, 0, b))
    for i in range(3):
        last, first = lengths(i)
        for b in range(1, first):
            src = own(i, 0, b)
            directs[i, b] = move(src, direct[i].at[b - 1], peer(i, 0, b))
    for i in range(3):
        last, first = lengths(i)
        for a in range(1, last):
            src = own(i, a, 0)
            terms = [src]
            for b in range(1, first):
                corners[i, a, b].wait_recv()
                terms.append(corner[i].at[a - 1, b - 1])
            add_into(mixed[i].at[a - 1], terms)
            routeds[i, a] = move(mixed[i].at[a - 1], routed[i].at[a - 1], peer(i, a, 0))
    ends = {}
    for i in range(3):
        last, first = lengths(i)
        terms = [own(i, 0, 0)]
        for b in range(1, first):
            directs[i, b].wait_recv()
            terms.append(direct[i].at[b - 1])
        for a in range(1, last):
            routeds[i, a].wait_recv()
            terms.append(routed[i].at[a - 1])
        add_into(total[i], terms)
        for o in range(1, deep):
            ends[i, o] = move(
                total[i].at[(z + o) % deep], lines[i].at[o - 1], at(sizes, x, core, (z + o) % deep, y)
            )
    for i in range(3):
        value = total[i][z].astype(F32)
        for o in range(1, deep):
            ends[i, o].wait_recv()
            value = value + lines[i][o - 1].astype(F32)
        outs[i][...] = value
    for copy in started:
        copy.wait_send()


def scatter_call(sizes, small, g_in, g_out):
    across, tall, deep = sizes
    copies = scatter_copies(sizes)
    parts = (small, g_in, g_out)
    vmem = pl.BlockSpec(memory_space=pltpu.VMEM)
    pieces = [p.shape[4:] for p in parts]
    kinds = [p.dtype for p in parts]

    def scratch(lead):
        return [pltpu.VMEM(lead(i) + pieces[i], kinds[i]) for i in range(3)]

    last = (across, across, tall)
    first = (tall, tall, across)
    grid = lambda i: (across, tall, deep)
    return pl.pallas_call(
        partial(scatter_kernel, sizes=sizes),
        out_shape=tuple(jax.ShapeDtypeStruct(p, F32) for p in pieces),
        in_specs=[vmem] * 3,
        out_specs=(vmem,) * 3,
        scratch_shapes=[
            *scratch(grid),
            *scratch(grid),
            *scratch(lambda i: (max(last[i] - 1, 1), max(first[i] - 1, 1), deep)),
            *scratch(lambda i: (max(last[i] - 1, 1), deep)),
            *scratch(lambda i: (max(first[i] - 1, 1), deep)),
            *scratch(lambda i: (max(last[i] - 1, 1), deep)),
            *scratch(lambda i: (deep,)),
            *scratch(lambda i: (max(deep - 1, 1),)),
            pltpu.SemaphoreType.DMA((copies,)),
            pltpu.SemaphoreType.DMA((copies,)),
        ],
        compiler_params=pltpu.CompilerParams(collective_id=1, has_side_effects=True, vmem_limit_bytes=60 << 20),
        name="scatter",
    )(*parts)


def on_device(
    mel_clips,
    live_counts,
    conv_weight,
    conv_bias,
    norm_gain,
    norm_shift,
    in_weight,
    in_bias,
    out_weight,
    out_bias,
    layer_scale,
    cotangent,
    *,
    sizes,
):
    shard, taps = conv_weight.shape
    kinds = taps + 5
    hid = in_weight.shape[1]
    devices = lax.axis_size(("dp", "fsdp"))
    chans = shard * devices
    wide = in_bias.shape[0]
    lead = (sizes[0], 2, sizes[2], sizes[1])

    lines = jnp.stack([conv_bias, norm_gain, norm_shift, out_bias, layer_scale])
    lines = jnp.pad(jnp.concatenate([conv_weight.T, lines]), ((0, 0), (0, 128 - shard)))
    last = jnp.pad(in_bias[None, :], ((0, 15 - kinds), (0, 128 - wide)))
    small, full_in, full_out = gather_call(sizes, jnp.concatenate([lines, last]), in_weight, out_weight)
    block_out, grad_clips, grad_in, grad_out, small = clip_call(
        live_counts.reshape(-1),
        mel_clips,
        cotangent,
        full_in.reshape(chans, hid),
        full_out.reshape(hid, chans),
        small.reshape(devices, 16, 128),
        taps,
    )
    small, grad_in, grad_out = scatter_call(
        sizes,
        small.reshape(lead + (16, 128)),
        grad_in.reshape(lead + in_weight.shape),
        grad_out.reshape(lead + out_weight.shape),
    )
    return (
        block_out,
        grad_clips,
        small[:taps, :shard].T,
        small[taps, :shard],
        small[taps + 1, :shard],
        small[taps + 2, :shard],
        grad_in,
        small[kinds, :wide],
        grad_out,
        small[taps + 3, :shard],
        small[taps + 4, :shard],
    )


def solution(mesh):
    both = ("dp", "fsdp")
    row, mat, cube = P(both), P(both, None), P(both, None, None)
    in_specs = (cube, mat, mat, row, row, row, mat, row, mat, row, row, cube)
    out_specs = (cube, cube, mat, row, row, row, mat, row, mat, row, row)
    body = partial(on_device, sizes=grid_of(mesh.shape))
    return jax.shard_map(body, mesh=mesh, in_specs=in_specs, out_specs=out_specs, check_vma=False)
```

```python
from functools import partial
import jax
import jax.numpy as jnp
from jax import lax
from jax.experimental import pallas as pl
from jax.experimental.pallas import tpu as pltpu
from jax.sharding import PartitionSpec as P

F32 = jnp.float32
BF16 = jnp.bfloat16
PAD = 8
ROOT_HALF = 0.7071067811865476
LOG2E = 1.4426950408889634
INV_ROOT_2PI = 0.3989422804014327


def dot_nn(a, b):
    return lax.dot_general(a, b, (((1,), (0,)), ((), ())), preferred_element_type=F32)


def dot_nt(a, b):
    return lax.dot_general(a, b, (((1,), (1,)), ((), ())), preferred_element_type=F32)


def fold8(v):
    total = v[0:8]
    for r in range(8, v.shape[0], 8):
        total = total + v[r : r + 8]
    return total


def clip_of(i, counts, slots):
    micros = counts.shape[0]
    lives = [counts[m] for m in range(micros)]
    count = lives[0]
    for m in range(1, micros):
        count = count + lives[m]
    alive = i < count
    rest = jnp.where(alive, i, i - count)
    clip = jnp.int32(0)
    start = jnp.int32(0)
    for m in range(micros):
        length = jnp.where(alive, lives[m], slots - lives[m])
        inside = jnp.logical_and(rest >= start, rest < start + length)
        first = m * slots + jnp.where(alive, 0, lives[m])
        clip = jnp.where(inside, first + rest - start, clip)
        start = start + length
    return clip


def lane_ids(rows):
    return lax.broadcasted_iota(jnp.int32, (rows, 128), 1)


def unpack_small(pieces_ref, kinds, rows_ref, ib_ref):
    devices = pieces_ref.shape[0]
    shard = rows_ref.shape[1] // devices
    wide = ib_ref.shape[1] // devices
    rows_ref[...] = jnp.zeros_like(rows_ref)
    ib_ref[...] = jnp.zeros_like(ib_ref)
    lane = lane_ids(8)
    for d in range(devices):
        piece = pieces_ref[d].astype(F32)
        at, off = divmod(d * shard, 128)
        rows_ref[:, at * 128 : at * 128 + 128] += pltpu.roll(piece, off, 1)
        at, off = divmod(d * wide, 128)
        moved = pltpu.roll(piece[8:16], off, 1)[kinds - 8 : kinds - 7]
        line = lane[0:1]
        ib_ref[0:1, at * 128 : at * 128 + 128] += jnp.where(line >= off, moved, 0.0)
        if off + wide > 128:
            ib_ref[0:1, at * 128 + 128 : at * 128 + 256] += jnp.where(line < off, moved, 0.0)


def pack_small(acc_small, acc_ib, rows_ref, small_ref):
    devices = small_ref.shape[0]
    kinds = acc_small.shape[0]
    shard = rows_ref.shape[1] // devices
    wide = acc_ib.shape[1] // devices
    for k in range(kinds):
        rows_ref[k : k + 1, :] = jnp.sum(acc_small[k], axis=0, keepdims=True)
    lane = lane_ids(16)
    bias = acc_ib[...]
    for d in range(devices):
        at, off = divmod(d * shard, 128)
        moved = pltpu.roll(rows_ref[:, at * 128 : at * 128 + 128], (128 - off) % 128, 1)
        small_ref[d] = jnp.where(lane < shard, moved, 0.0)
        at, off = divmod(d * wide, 128)
        moved = pltpu.roll(bias[:, at * 128 : at * 128 + 128], (128 - off) % 128, 1)
        if off + wide > 128:
            later = pltpu.roll(bias[:, at * 128 + 128 : at * 128 + 256], 128 - off, 1)
            moved = jnp.where(lane[0:8] < 128 - off, moved, later)
        moved = jnp.where(lane[0:8] < wide, moved, 0.0)
        small_ref[d, kinds : kinds + 1, :] = jnp.sum(moved, axis=0, keepdims=True)


def clip_kernel(
    counts_ref,
    order_ref,
    x_ref,
    dy_ref,
    xn_ref,
    dyn_ref,
    w_in_ref,
    w_out_ref,
    pieces_ref,
    out_ref,
    gx_ref,
    gin_ref,
    gout_ref,
    small_ref,
    rows_ref,
    ib_ref,
    xp,
    gm,
    xh,
    rs,
    left,
    acts,
    gob,
    nb,
    gn,
    raw,
    acc,
    acc_small,
    acc_ib,
    *,
    taps,
    hid_chunk,
    row_chunk,
    parts,
):
    step = pl.program_id(0)
    _, groups, frames, lanes = xh.shape
    chans = groups * lanes
    hid = acts.shape[2]
    margin = (taps - 1) // 2
    gain, shift, obias, scale = taps + 1, taps + 2, taps + 3, taps + 4
    span = [slice(g * lanes, (g + 1) * lanes) for g in range(groups)]
    now = step % 2
    then = 1 - now
    live_count = counts_ref[0]
    for m in range(1, counts_ref.shape[0]):
        live_count = live_count + counts_ref[m]
    live = step < live_count

    def row(i, g):
        return rows_ref[i : i + 1, span[g]]

    def total(blocks):
        added = blocks[0]
        for block in blocks[1:]:
            added = added + block
        return jnp.sum(added, axis=-1, keepdims=True) * (1.0 / chans)

    def stage(x_in, to):
        for g in range(groups):
            xp[to, g, PAD : PAD + frames, :] = x_in[0, :, span[g]].astype(F32)

    def begin(dy_in, to, start, size):
        for r in range(0, size, row_chunk):
            low = start + r
            at_rows = pl.ds(low, row_chunk)
            mixed = []
            for g in range(groups):
                m = row(taps, g) + xp[to, g, pl.ds(low + (PAD - margin), row_chunk), :] * row(0, g)
                for k in range(1, taps):
                    m = m + xp[to, g, pl.ds(low + (PAD - margin + k), row_chunk), :] * row(k, g)
                mixed.append(m)
            mean = total(mixed)
            center = [m - mean for m in mixed]
            inv = lax.rsqrt(total([c * c for c in center]) + 1e-06)
            rs[to, at_rows, :] = jnp.broadcast_to(inv, (row_chunk, lanes))
            for g in range(groups):
                xhat = center[g] * inv
                xh[to, g, at_rows, :] = xhat
                nb[to, at_rows, span[g]] = (xhat * row(gain, g) + row(shift, g)).astype(BF16)
                gob[to, at_rows, span[g]] = (dy_in[0, at_rows, span[g]].astype(F32) * row(scale, g)).astype(BF16)

    def turn(to):
        left[to, 0] = gob[to].T
        left[to, 1] = nb[to].T

    @pl.when(step == 0)
    def _():
        unpack_small(pieces_ref, taps + 5, rows_ref, ib_ref)
        acc[...] = jnp.zeros_like(acc)
        acc_small[...] = jnp.zeros_like(acc_small)
        acc_ib[...] = jnp.zeros_like(acc_ib)
        edge = jnp.zeros((2, groups, PAD, lanes), F32)
        xp[:, :, 0:PAD, :] = edge
        xp[:, :, PAD + frames :, :] = edge
        gm[:, 0:PAD, :] = edge[0]
        gm[:, PAD + frames :, :] = edge[0]
        stage(x_ref, 0)
        begin(dy_ref, 0, 0, frames)
        turn(0)

    @pl.when(jnp.logical_not(live))
    def _():
        out_ref[...] = x_ref[...]
        gx_ref[...] = dy_ref[...]

    @pl.when(live)
    def _():
        stage(xn_ref, then)
        for j in range(0, hid, hid_chunk):
            cols = slice(j, j + hid_chunk)
            h = dot_nn(nb[now], w_in_ref[:, cols]) + ib_ref[0:1, cols]
            u = h * ROOT_HALF
            cdf = 0.5 * lax.erf(u) + 0.5
            slope = cdf + h * (jnp.exp2(u * u * (-LOG2E)) * INV_ROOT_2PI)
            acts[0, :, cols] = (h * cdf).astype(BF16)
            ga = dot_nt(gob[now], w_out_ref[cols, :])
            gh = (ga * slope).astype(BF16)
            acts[1, :, cols] = gh
            acc_ib[:, cols] += fold8(gh.astype(F32))

        wide = 256
        tall = frames // (2 * (chans // wide))
        for c in range(0, chans, wide):
            spot = 2 * (c // wide) * tall
            gn[:, c : c + wide] = dot_nt(acts[1], w_in_ref[c : c + wide, :])
            begin(dyn_ref, then, spot, tall)
            raw[:, c : c + wide] = dot_nn(acts[0], w_out_ref[:, c : c + wide])
            begin(dyn_ref, then, spot + tall, tall)
        turn(then)

        rows_each = frames // parts
        units = 2 * (hid // hid_chunk)

        def norm_back(base):
            at_rows = pl.ds(base, rows_each)
            hats = [xh[now, g, at_rows, :] for g in range(groups)]
            grads = [gn[at_rows, span[g]] for g in range(groups)]
            gained = []
            for g in range(groups):
                acc_small[shift, :, span[g]] += fold8(grads[g])
                acc_small[gain, :, span[g]] += fold8(grads[g] * hats[g])
                gained.append(grads[g] * row(gain, g))
            mean = total(gained)
            slant = total([v * h for v, h in zip(gained, hats)])
            inv = rs[now, at_rows, :]
            for g in range(groups):
                gmix = inv * (gained[g] - mean - hats[g] * slant)
                acc_small[taps, :, span[g]] += fold8(gmix)
                gm[g, pl.ds(base + PAD, rows_each), :] = gmix

        def finish(base):
            at_rows = pl.ds(base, rows_each)
            for g in range(groups):
                o = raw[at_rows, span[g]] + row(obias, g)
                dy = dy_ref[0, at_rows, span[g]].astype(F32)
                acc_small[scale, :, span[g]] += fold8(dy * o)
                acc_small[obias, :, span[g]] += fold8(gob[now, at_rows, span[g]].astype(F32))
                x = xp[now, g, pl.ds(base + PAD, rows_each), :]
                out_ref[0, at_rows, span[g]] = (x + o * row(scale, g)).astype(BF16)

        def conv_back(base):
            at_rows = pl.ds(base, rows_each)
            for g in range(groups):
                x = xp[now, g, pl.ds(base + PAD, rows_each), :]
                grad = dy_ref[0, at_rows, span[g]].astype(F32)
                for k in range(taps):
                    moved = gm[g, pl.ds(base + (PAD + margin - k), rows_each), :]
                    grad = grad + moved * row(k, g)
                    acc_small[k, :, span[g]] += fold8(moved * x)
                gx_ref[0, at_rows, span[g]] = grad.astype(BF16)

        def weights(unit):
            side, place = unit % 2, unit // 2
            cols = slice(place * hid_chunk, (place + 1) * hid_chunk)
            acc[side, :, cols] += dot_nn(left[now, side], acts[side, :, cols])

        done = 0
        for i in range(parts):
            upto = units * (i + 1) // parts
            norm_back(i * rows_each)
            for unit in range(done, upto):
                weights(unit)
            done = upto
            finish(i * rows_each)
            if i > 0:
                conv_back((i - 1) * rows_each)
        conv_back(frames - rows_each)

    @pl.when(step == pl.num_programs(0) - 1)
    def _():
        gin_ref[...] = acc[1].astype(gin_ref.dtype)
        for j in range(0, hid, 128):
            gout_ref[j : j + 128, :] = acc[0, :, j : j + 128].T.astype(gout_ref.dtype)
        pack_small(acc_small, acc_ib, rows_ref, small_ref)


def clip_call(counts, order, x, dy, w_in, w_out, pieces, taps, grad_dtype=BF16):
    clips, frames, chans = x.shape
    hid = w_in.shape[1]
    kinds = taps + 5

    def clip_spec(ahead):
        def index(i, counts, order):
            return order[jnp.minimum(i + ahead, clips - 1)], 0, 0

        return pl.BlockSpec((1, frames, chans), index)

    def whole(shape):
        return pl.BlockSpec(shape, lambda i, counts, order: (0,) * len(shape), pipeline_mode=pl.Buffered(1))

    groups = chans // 128
    return pl.pallas_call(
        partial(clip_kernel, taps=taps, hid_chunk=256, row_chunk=32, parts=8),
        out_shape=(
            jax.ShapeDtypeStruct(x.shape, BF16),
            jax.ShapeDtypeStruct(x.shape, BF16),
            jax.ShapeDtypeStruct((chans, hid), grad_dtype),
            jax.ShapeDtypeStruct((hid, chans), grad_dtype),
            jax.ShapeDtypeStruct(pieces.shape, F32),
        ),
        grid_spec=pltpu.PrefetchScalarGridSpec(
            num_scalar_prefetch=2,
            grid=(clips,),
            in_specs=[
                clip_spec(0),
                clip_spec(0),
                clip_spec(1),
                clip_spec(1),
                whole((chans, hid)),
                whole((hid, chans)),
                whole(pieces.shape),
            ],
            out_specs=(
                clip_spec(0),
                clip_spec(0),
                whole((chans, hid)),
                whole((hid, chans)),
                whole(pieces.shape),
            ),
            scratch_shapes=[
                pltpu.VMEM((16, chans), F32),
                pltpu.VMEM((8, hid), F32),
                pltpu.VMEM((2, groups, frames + 2 * PAD, 128), F32),
                pltpu.VMEM((groups, frames + 2 * PAD, 128), F32),
                pltpu.VMEM((2, groups, frames, 128), F32),
                pltpu.VMEM((2, frames, 128), F32),
                pltpu.VMEM((2, 2, chans, frames), BF16),
                pltpu.VMEM((2, frames, hid), BF16),
                pltpu.VMEM((2, frames, chans), BF16),
                pltpu.VMEM((2, frames, chans), BF16),
                pltpu.VMEM((frames, chans), F32),
                pltpu.VMEM((frames, chans), F32),
                pltpu.VMEM((2, chans, hid), F32),
                pltpu.VMEM((kinds, 8, chans), F32),
                pltpu.VMEM((8, hid), F32),
            ],
        ),
        compiler_params=pltpu.CompilerParams(vmem_limit_bytes=60 << 20),
        name="clips",
    )(counts, order, x, dy, x, dy, w_in, w_out, pieces)


MESH = pl.DeviceIdType.MESH


def grid_of(mesh_shape):
    across = mesh_shape["dp"] // 2
    deep = mesh_shape["fsdp"]
    tall = across if deep % across == 0 else 1
    return across, tall, deep // tall


def place(sizes):
    dp = lax.axis_index("dp")
    fsdp = lax.axis_index("fsdp")
    return dp // 2, dp % 2, fsdp // sizes[1], fsdp % sizes[1]


def at(sizes, x, core, z, y):
    return {"dp": x * 2 + core, "fsdp": z * sizes[1] + y}


def partners(sizes):
    x, core, z, y = place(sizes)
    across, tall, deep = sizes
    found = [at(sizes, x, 1 - core, z, y)]
    found += [at(sizes, (x + o) % across, core, z, y) for o in range(1, across)]
    found += [at(sizes, x, core, z, (y + o) % tall) for o in range(1, tall)]
    found += [at(sizes, x, core, (z + o) % deep, y) for o in range(1, deep)]
    return found


def greet(sizes):
    barrier = pltpu.get_barrier_semaphore()
    others = partners(sizes)
    for other in others:
        pl.semaphore_signal(barrier, inc=1, device_id=other, device_id_type=MESH)
    pl.semaphore_wait(barrier, len(others))


def send(src, dst, send_sems, recv_sems, slot, device):
    copy = pltpu.make_async_remote_copy(
        src_ref=src,
        dst_ref=dst,
        send_sem=send_sems.at[slot],
        recv_sem=recv_sems.at[slot],
        device_id=device,
        device_id_type=MESH,
    )
    copy.start()
    return copy


class Slots:
    def __init__(self):
        self.used = 0

    def take(self):
        self.used += 1
        return self.used - 1


def streams_of(refs_in, refs_full, cuts):
    widths = [r.shape[-1] for r in refs_in]
    found = [[(0, slice(0, widths[0]), True)]] + [[] for _ in range(cuts - 1)]
    for c in range(cuts):
        for i, x_first in ((1, True), (2, False)):
            each = widths[i] // cuts
            found[c].append((i, slice(c * each, (c + 1) * each), x_first))
    return found


def copies_of(sizes, streams):
    across, tall, deep = sizes
    columns = across * tall
    return streams * ((deep - 1) + (columns - 1) + columns)


def gather_kernel(*refs, sizes, cuts, slots, kinds):
    across, tall, deep = sizes
    counts_ref, conv_ref = refs[0:2]
    vectors = refs[2:7]
    bias_ref, in_ref, out_ref, full_small, full_in, full_out, order_ref = refs[7:14]
    tile, small_ref, send_sems, recv_sems, local_sems = refs[14:]
    x, core, z, y = place(sizes)
    slots_used = Slots()
    started = []
    greet(sizes)
    tile[...] = jnp.zeros_like(tile)
    taps, shard = conv_ref.shape
    tile[0:taps, 0:shard] = conv_ref[...].astype(F32)
    for k, vector in enumerate(vectors):
        tile[taps + k : taps + k + 1, 0:shard] = vector[...].astype(F32)
    tile[kinds : kinds + 1, 0 : bias_ref.shape[1]] = bias_ref[...].astype(F32)
    small_ref[...] = tile[...].astype(BF16)

    own = (small_ref, in_ref, out_ref)
    full = (full_small, full_in, full_out)
    groups = streams_of(own, full, cuts)

    def move(src, dst, device):
        copy = send(src, dst, send_sems, recv_sems, slots_used.take(), device)
        started.append(copy)
        return copy

    def column(stream, cx, cy):
        i, cols, _ = stream
        return full[i].at[cx, core, :, cy, :, cols]

    def along(stream, cx, cy, device):
        ref = column(stream, cx, cy)
        return move(ref, ref, device)

    def beside(stream, cx, cy):
        sides.append(along(stream, cx, cy, at(sizes, x, 1 - core, z, y)))

    keeps = []
    lines = {}
    sides = []
    for i in (1, 2, 0):
        keep = pltpu.make_async_copy(own[i], full[i].at[x, core, z, y], local_sems.at[i])
        keep.start()
        keeps.append(keep)
    for c in range(cuts):
        for s, (i, cols, _) in enumerate(groups[c]):
            lines[c, s] = [
                move(
                    own[i].at[:, cols],
                    full[i].at[x, core, z, y, :, cols],
                    at(sizes, x, core, (z + o) % deep, y),
                )
                for o in range(1, deep)
            ]
    for k in range(order_ref.shape[0]):
        order_ref[k] = clip_of(jnp.int32(k), counts_ref, slots)
    for keep in keeps:
        keep.wait()
    firsts = {}
    for c in range(cuts):
        for s, stream in enumerate(groups[c]):
            for copy in lines[c, s]:
                copy.wait_recv()
            firsts[c, s] = (
                [along(stream, x, y, at(sizes, (x + o) % across, core, z, y)) for o in range(1, across)],
                [along(stream, x, y, at(sizes, x, core, z, (y + o) % tall)) for o in range(1, tall)],
            )
            beside(stream, x, y)
    passed = {}
    for c in range(cuts):
        for s, stream in enumerate(groups[c]):
            along_x, along_y = firsts[c, s]
            lead, other = (along_x, along_y) if stream[2] else (along_y, along_x)
            passed[c, s] = []
            for o, copy in enumerate(lead, 1):
                copy.wait_recv()
                if stream[2]:
                    cx, cy = (x - o + across) % across, y
                    goals = [at(sizes, x, core, z, (y + p) % tall) for p in range(1, tall)]
                else:
                    cx, cy = x, (y - o + tall) % tall
                    goals = [at(sizes, (x + p) % across, core, z, y) for p in range(1, across)]
                passed[c, s].append([along(stream, cx, cy, goal) for goal in goals])
                beside(stream, cx, cy)
            for o, copy in enumerate(other, 1):
                copy.wait_recv()
                if stream[2]:
                    beside(stream, x, (y - o + tall) % tall)
                else:
                    beside(stream, (x - o + across) % across, y)
    for c in range(cuts):
        for s, stream in enumerate(groups[c]):
            for o, goals in enumerate(passed[c, s], 1):
                for p, copy in enumerate(goals, 1):
                    copy.wait_recv()
                    dx, dy = (o, p) if stream[2] else (p, o)
                    beside(stream, (x - dx + across) % across, (y - dy + tall) % tall)
    for copy in sides:
        copy.wait_recv()
    for copy in started:
        copy.wait_send()


def gather_call(sizes, counts, clips, conv, vectors, bias, w_in, w_out):
    across, tall, deep = sizes
    cuts = 2
    copies = copies_of(sizes, 2 * cuts + 1)
    vmem = pl.BlockSpec(memory_space=pltpu.VMEM)
    smem = pl.BlockSpec(memory_space=pltpu.SMEM)
    shapes = ((16, 128), w_in.shape, w_out.shape)
    kinds = conv.shape[0] + len(vectors)
    return pl.pallas_call(
        partial(gather_kernel, sizes=sizes, cuts=cuts, slots=clips // counts.shape[0], kinds=kinds),
        out_shape=tuple(jax.ShapeDtypeStruct((across, 2, deep, tall) + s, BF16) for s in shapes)
        + (jax.ShapeDtypeStruct((clips,), jnp.int32),),
        in_specs=[smem] + [vmem] * (len(vectors) + 4),
        out_specs=(pl.BlockSpec(memory_space=pl.ANY),) * 3 + (smem,),
        scratch_shapes=[
            pltpu.VMEM((16, 128), F32),
            pltpu.VMEM((16, 128), BF16),
            pltpu.SemaphoreType.DMA((copies,)),
            pltpu.SemaphoreType.DMA((copies,)),
            pltpu.SemaphoreType.DMA((3,)),
        ],
        compiler_params=pltpu.CompilerParams(collective_id=0, has_side_effects=True),
        name="gather",
    )(counts, conv, *vectors, bias, w_in, w_out)


def add_into(dst, terms):
    def block(k, carry):
        total = terms[0][k].astype(F32)
        for term in terms[1:]:
            total = total + term[k].astype(F32)
        dst[k] = total.astype(dst.dtype)
        return carry

    lax.fori_loop(0, dst.shape[0], block, 0)


def scatter_kernel(*refs, sizes, cuts):
    across, tall, deep = sizes
    parts = refs[0:3]
    outs = refs[3:6]
    side = refs[6:9]
    held = refs[9:12]
    corner = refs[12:15]
    mixed = refs[15:18]
    direct = refs[18:21]
    routed = refs[21:24]
    total = refs[24:27]
    lines = refs[27:30]
    send_sems, recv_sems = refs[30:32]
    x, core, z, y = place(sizes)
    slots_used = Slots()
    greet(sizes)
    started = []
    groups = streams_of(parts, outs, cuts)

    def move(src, dst, device):
        copy = send(src, dst, send_sems, recv_sems, slots_used.take(), device)
        started.append(copy)
        return copy

    def far(stream, a, b):
        if stream[2]:
            return (x + a) % across, (y + b) % tall
        return (x + b) % across, (y + a) % tall

    def lengths(stream):
        return (across, tall) if stream[2] else (tall, across)

    def peer(stream, a, b):
        cx, cy = far(stream, a, b)
        return at(sizes, cx, core, z, cy)

    def of(group, stream, *index):
        i, cols, _ = stream
        return group[i].at[index + (slice(None), slice(None), cols)]

    crossings = {}

    def cross(c, s, a, b):
        stream = groups[c][s]
        cx, cy = far(stream, a, b)
        i, cols, _ = stream
        crossings[c, s, a, b] = move(
            parts[i].at[cx, 1 - core, :, cy, :, cols],
            of(side, stream, cx, cy),
            at(sizes, x, 1 - core, z, y),
        )

    every = [(c, s) for c in range(cuts) for s in range(len(groups[c]))]
    for c in range(cuts):
        for kind in range(4):
            for s, stream in enumerate(groups[c]):
                last, first = lengths(stream)
                if kind == 0:
                    steps = [(a, b) for a in range(1, last) for b in range(1, first)]
                elif kind == 1:
                    steps = [(0, b) for b in range(1, first)]
                elif kind == 2:
                    steps = [(a, 0) for a in range(1, last)]
                else:
                    steps = [(0, 0)]
                for a, b in steps:
                    cross(c, s, a, b)

    def own(c, s, a, b):
        stream = groups[c][s]
        i, cols, _ = stream
        cx, cy = far(stream, a, b)
        crossings[c, s, a, b].wait_recv()
        add_into(of(held, stream, cx, cy), [parts[i].at[cx, core, :, cy, :, cols], of(side, stream, cx, cy)])
        return of(held, stream, cx, cy)

    corners, directs, routeds, ends = {}, {}, {}, {}

    def send_corners(c):
        for s, stream in enumerate(groups[c]):
            last, first = lengths(stream)
            for a in range(1, last):
                for b in range(1, first):
                    src = own(c, s, a, b)
                    corners[c, s, a, b] = move(src, of(corner, stream, a - 1, b - 1), peer(stream, 0, b))

    def send_directs(c):
        for s, stream in enumerate(groups[c]):
            for b in range(1, lengths(stream)[1]):
                src = own(c, s, 0, b)
                directs[c, s, b] = move(src, of(direct, stream, b - 1), peer(stream, 0, b))

    def send_routeds(c):
        for s, stream in enumerate(groups[c]):
            last, first = lengths(stream)
            for a in range(1, last):
                terms = [own(c, s, a, 0)]
                for b in range(1, first):
                    corners[c, s, a, b].wait_recv()
                    terms.append(of(corner, stream, a - 1, b - 1))
                add_into(of(mixed, stream, a - 1), terms)
                routeds[c, s, a] = move(of(mixed, stream, a - 1), of(routed, stream, a - 1), peer(stream, a, 0))

    def send_ends(c):
        for s, stream in enumerate(groups[c]):
            i, cols, _ = stream
            last, first = lengths(stream)
            terms = [own(c, s, 0, 0)]
            for b in range(1, first):
                directs[c, s, b].wait_recv()
                terms.append(of(direct, stream, b - 1))
            for a in range(1, last):
                routeds[c, s, a].wait_recv()
                terms.append(of(routed, stream, a - 1))
            add_into(of(total, stream), terms)
            for o in range(1, deep):
                ends[c, s, o] = move(
                    total[i].at[(z + o) % deep, :, cols],
                    lines[i].at[o - 1, :, cols],
                    at(sizes, x, core, (z + o) % deep, y),
                )

    send_corners(0)
    send_directs(0)
    for c in range(1, cuts):
        send_corners(c)
        send_routeds(c - 1)
        send_directs(c)
    send_routeds(cuts - 1)
    for c in range(cuts):
        send_ends(c)
    for c, s in every:
        i, cols, _ = groups[c][s]
        value = total[i][z, :, cols].astype(F32)
        for o in range(1, deep):
            ends[c, s, o].wait_recv()
            value = value + lines[i][o - 1, :, cols].astype(F32)
        outs[i][:, cols] = value
    for copy in started:
        copy.wait_send()


def scatter_call(sizes, small, g_in, g_out):
    across, tall, deep = sizes
    cuts = 2
    copies = copies_of(sizes, 2 * cuts + 1)
    parts = (small, g_in, g_out)
    vmem = pl.BlockSpec(memory_space=pltpu.VMEM)
    pieces = [p.shape[4:] for p in parts]
    kinds = [p.dtype for p in parts]

    def scratch(lead):
        return [pltpu.VMEM(lead(i) + pieces[i], kinds[i]) for i in range(3)]

    last = (across, across, tall)
    first = (tall, tall, across)
    grid = lambda i: (across, tall, deep)
    return pl.pallas_call(
        partial(scatter_kernel, sizes=sizes, cuts=cuts),
        out_shape=tuple(jax.ShapeDtypeStruct(p, F32) for p in pieces),
        in_specs=[vmem] * 3,
        out_specs=(vmem,) * 3,
        scratch_shapes=[
            *scratch(grid),
            *scratch(grid),
            *scratch(lambda i: (max(last[i] - 1, 1), max(first[i] - 1, 1), deep)),
            *scratch(lambda i: (max(last[i] - 1, 1), deep)),
            *scratch(lambda i: (max(first[i] - 1, 1), deep)),
            *scratch(lambda i: (max(last[i] - 1, 1), deep)),
            *scratch(lambda i: (deep,)),
            *scratch(lambda i: (max(deep - 1, 1),)),
            pltpu.SemaphoreType.DMA((copies,)),
            pltpu.SemaphoreType.DMA((copies,)),
        ],
        compiler_params=pltpu.CompilerParams(collective_id=1, has_side_effects=True, vmem_limit_bytes=60 << 20),
        name="scatter",
    )(*parts)


def close_kernel(small_ref, in_ref, out_ref, *results, taps):
    conv, bias, g_in, g_out = results[0], results[6], results[7], results[8]
    shard = conv.shape[1]
    conv[...] = small_ref[0:taps, 0:shard]
    for k in range(5):
        results[1 + k][...] = small_ref[taps + k : taps + k + 1, 0:shard]
    bias[...] = small_ref[taps + 5 : taps + 6, 0 : bias.shape[1]]
    g_in[...] = in_ref[...]
    g_out[...] = out_ref[...]


def close_call(small, g_in, g_out, taps, shard, wide):
    shapes = [(taps, shard)] + [(1, shard)] * 5 + [(1, wide), g_in.shape, g_out.shape]
    return pl.pallas_call(
        partial(close_kernel, taps=taps),
        out_shape=tuple(jax.ShapeDtypeStruct(s, F32) for s in shapes),
        name="close",
    )(small, g_in, g_out)


def on_device(
    mel_clips,
    live_counts,
    conv_weight,
    conv_bias,
    norm_gain,
    norm_shift,
    in_weight,
    in_bias,
    out_weight,
    out_bias,
    layer_scale,
    cotangent,
    *,
    sizes,
):
    shard, taps = conv_weight.shape
    hid = in_weight.shape[1]
    devices = lax.axis_size(("dp", "fsdp"))
    chans = shard * devices
    wide = in_bias.shape[0]
    lead = (sizes[0], 2, sizes[2], sizes[1])

    counts = live_counts.reshape(-1)
    vectors = [v[None, :] for v in (conv_bias, norm_gain, norm_shift, out_bias, layer_scale)]
    small, full_in, full_out, order = gather_call(
        sizes, counts, mel_clips.shape[0], conv_weight.T, vectors, in_bias[None, :], in_weight, out_weight
    )
    block_out, grad_clips, grad_in, grad_out, small = clip_call(
        counts,
        order,
        mel_clips,
        cotangent,
        full_in.reshape(chans, hid),
        full_out.reshape(hid, chans),
        small.reshape(devices, 16, 128),
        taps,
    )
    small, grad_in, grad_out = scatter_call(
        sizes,
        small.reshape(lead + (16, 128)),
        grad_in.reshape(lead + in_weight.shape),
        grad_out.reshape(lead + out_weight.shape),
    )
    conv, cbias, gain, shift, obias, scale, ibias, grad_in, grad_out = close_call(
        small, grad_in, grad_out, taps, shard, wide
    )
    vector = lambda v: v.reshape(-1)
    return (
        block_out,
        grad_clips,
        conv.T,
        vector(cbias),
        vector(gain),
        vector(shift),
        grad_in,
        vector(ibias),
        grad_out,
        vector(obias),
        vector(scale),
    )


def solution(mesh):
    both = ("dp", "fsdp")
    row, mat, cube = P(both), P(both, None), P(both, None, None)
    in_specs = (cube, mat, mat, row, row, row, mat, row, mat, row, row, cube)
    out_specs = (cube, cube, mat, row, row, row, mat, row, mat, row, row)
    body = partial(on_device, sizes=grid_of(mesh.shape))
    return jax.shard_map(body, mesh=mesh, in_specs=in_specs, out_specs=out_specs, check_vma=False)
```

```python
from functools import partial
import jax
import jax.numpy as jnp
from jax import lax
from jax.experimental import pallas as pl
from jax.experimental.pallas import tpu as pltpu
from jax.sharding import PartitionSpec as P

F32 = jnp.float32
BF16 = jnp.bfloat16
PAD = 8
ONES = 16
ROOT_HALF = 0.7071067811865476
LOG2E = 1.4426950408889634
INV_ROOT_2PI = 0.3989422804014327


def dot_nn(a, b):
    return lax.dot_general(a, b, (((1,), (0,)), ((), ())), preferred_element_type=F32)


def dot_nt(a, b):
    return lax.dot_general(a, b, (((1,), (1,)), ((), ())), preferred_element_type=F32)


def fold8(v):
    total = v[0:8]
    for r in range(8, v.shape[0], 8):
        total = total + v[r : r + 8]
    return total


def clip_of(i, counts, slots):
    micros = counts.shape[0]
    lives = [counts[m] for m in range(micros)]
    count = lives[0]
    for m in range(1, micros):
        count = count + lives[m]
    alive = i < count
    rest = jnp.where(alive, i, i - count)
    clip = jnp.int32(0)
    start = jnp.int32(0)
    for m in range(micros):
        length = jnp.where(alive, lives[m], slots - lives[m])
        inside = jnp.logical_and(rest >= start, rest < start + length)
        first = m * slots + jnp.where(alive, 0, lives[m])
        clip = jnp.where(inside, first + rest - start, clip)
        start = start + length
    return clip


def lane_ids(rows):
    return lax.broadcasted_iota(jnp.int32, (rows, 128), 1)


def unpack_small(pieces_ref, kinds, rows_ref, ib_ref):
    devices = pieces_ref.shape[0]
    shard = rows_ref.shape[1] // devices
    wide = ib_ref.shape[1] // devices
    rows_ref[...] = jnp.zeros_like(rows_ref)
    ib_ref[...] = jnp.zeros_like(ib_ref)
    lane = lane_ids(8)
    for d in range(devices):
        piece = pieces_ref[d].astype(F32)
        at, off = divmod(d * shard, 128)
        rows_ref[:, at * 128 : at * 128 + 128] += pltpu.roll(piece, off, 1)
        at, off = divmod(d * wide, 128)
        moved = pltpu.roll(piece[8:16], off, 1)[kinds - 8 : kinds - 7]
        line = lane[0:1]
        ib_ref[0:1, at * 128 : at * 128 + 128] += jnp.where(line >= off, moved, 0.0)
        if off + wide > 128:
            ib_ref[0:1, at * 128 + 128 : at * 128 + 256] += jnp.where(line < off, moved, 0.0)


def pack_small(acc_small, bias, rows_ref, small_ref):
    devices = small_ref.shape[0]
    kinds = acc_small.shape[0]
    shard = rows_ref.shape[1] // devices
    wide = bias.shape[1] // devices
    for k in range(kinds):
        rows_ref[k : k + 1, :] = jnp.sum(acc_small[k], axis=0, keepdims=True)
    lane = lane_ids(16)
    for d in range(devices):
        at, off = divmod(d * shard, 128)
        moved = pltpu.roll(rows_ref[:, at * 128 : at * 128 + 128], (128 - off) % 128, 1)
        small_ref[d] = jnp.where(lane < shard, moved, 0.0)
        at, off = divmod(d * wide, 128)
        moved = pltpu.roll(bias[:, at * 128 : at * 128 + 128], (128 - off) % 128, 1)
        if off + wide > 128:
            later = pltpu.roll(bias[:, at * 128 + 128 : at * 128 + 256], 128 - off, 1)
            moved = jnp.where(lane[0:8] < 128 - off, moved, later)
        moved = jnp.where(lane[0:8] < wide, moved, 0.0)
        small_ref[d, kinds : kinds + 1, :] = jnp.sum(moved, axis=0, keepdims=True)


def clip_kernel(
    counts_ref,
    order_ref,
    x_ref,
    dy_ref,
    xn_ref,
    dyn_ref,
    w_in_ref,
    w_out_ref,
    pieces_ref,
    out_ref,
    gx_ref,
    gin_ref,
    gout_ref,
    small_ref,
    rows_ref,
    ib_ref,
    xp,
    gm,
    xh,
    rs,
    left,
    acts,
    gob,
    nb,
    gn,
    raw,
    acc,
    acc_small,
    *,
    taps,
    hid_chunk,
    row_chunk,
    parts,
):
    step = pl.program_id(0)
    _, groups, frames, lanes = xh.shape
    chans = groups * lanes
    hid = acts.shape[2]
    margin = (taps - 1) // 2
    gain, shift, obias, scale = taps + 1, taps + 2, taps + 3, taps + 4
    span = [slice(g * lanes, (g + 1) * lanes) for g in range(groups)]
    now = step % 2
    then = 1 - now
    live_count = counts_ref[0]
    for m in range(1, counts_ref.shape[0]):
        live_count = live_count + counts_ref[m]
    live = step < live_count

    def row(i, g):
        return rows_ref[i : i + 1, span[g]]

    def total(blocks):
        added = blocks[0]
        for block in blocks[1:]:
            added = added + block
        return jnp.sum(added, axis=-1, keepdims=True) * (1.0 / chans)

    def stage(x_in, to):
        for g in range(groups):
            xp[to, g, PAD : PAD + frames, :] = x_in[0, :, span[g]].astype(F32)

    def begin(dy_in, to, start, size):
        for r in range(0, size, row_chunk):
            low = start + r
            at_rows = pl.ds(low, row_chunk)
            mixed = []
            for g in range(groups):
                m = row(taps, g) + xp[to, g, pl.ds(low + (PAD - margin), row_chunk), :] * row(0, g)
                for k in range(1, taps):
                    m = m + xp[to, g, pl.ds(low + (PAD - margin + k), row_chunk), :] * row(k, g)
                mixed.append(m)
            mean = total(mixed)
            center = [m - mean for m in mixed]
            inv = lax.rsqrt(total([c * c for c in center]) + 1e-06)
            rs[to, at_rows, :] = jnp.broadcast_to(inv, (row_chunk, lanes))
            for g in range(groups):
                xhat = center[g] * inv
                xh[to, g, at_rows, :] = xhat
                nb[to, at_rows, span[g]] = (xhat * row(gain, g) + row(shift, g)).astype(BF16)
                gob[to, at_rows, span[g]] = (dy_in[0, at_rows, span[g]].astype(F32) * row(scale, g)).astype(BF16)

    def turn(to):
        left[to, 0, 0:chans] = gob[to].T
        left[to, 1, 0:chans] = nb[to].T

    @pl.when(step == 0)
    def _():
        unpack_small(pieces_ref, taps + 5, rows_ref, ib_ref)
        acc[...] = jnp.zeros_like(acc)
        acc_small[...] = jnp.zeros_like(acc_small)
        left[:, :, chans:, :] = jnp.ones((2, 2, ONES, frames), BF16)
        edge = jnp.zeros((2, groups, PAD, lanes), F32)
        xp[:, :, 0:PAD, :] = edge
        xp[:, :, PAD + frames :, :] = edge
        gm[:, 0:PAD, :] = edge[0]
        gm[:, PAD + frames :, :] = edge[0]
        stage(x_ref, 0)
        begin(dy_ref, 0, 0, frames)
        turn(0)

    @pl.when(jnp.logical_not(live))
    def _():
        out_ref[...] = x_ref[...]
        gx_ref[...] = dy_ref[...]

    @pl.when(live)
    def _():
        stage(xn_ref, then)
        for j in range(0, hid, hid_chunk):
            cols = slice(j, j + hid_chunk)
            h = dot_nn(nb[now], w_in_ref[:, cols]) + ib_ref[0:1, cols]
            u = h * ROOT_HALF
            cdf = 0.5 * lax.erf(u) + 0.5
            slope = cdf + h * (jnp.exp2(u * u * (-LOG2E)) * INV_ROOT_2PI)
            acts[0, :, cols] = (h * cdf).astype(BF16)
            ga = dot_nt(gob[now], w_out_ref[cols, :])
            acts[1, :, cols] = (ga * slope).astype(BF16)

        wide = 256
        tall = frames // (2 * (chans // wide))
        for c in range(0, chans, wide):
            spot = 2 * (c // wide) * tall
            gn[:, c : c + wide] = dot_nt(acts[1], w_in_ref[c : c + wide, :])
            begin(dyn_ref, then, spot, tall)
            raw[:, c : c + wide] = dot_nn(acts[0], w_out_ref[:, c : c + wide])
            begin(dyn_ref, then, spot + tall, tall)
        turn(then)

        rows_each = frames // parts
        units = 2 * (hid // hid_chunk)

        def norm_back(base):
            at_rows = pl.ds(base, rows_each)
            hats = [xh[now, g, at_rows, :] for g in range(groups)]
            grads = [gn[at_rows, span[g]] for g in range(groups)]
            gained = []
            for g in range(groups):
                acc_small[shift, :, span[g]] += fold8(grads[g])
                acc_small[gain, :, span[g]] += fold8(grads[g] * hats[g])
                gained.append(grads[g] * row(gain, g))
            mean = total(gained)
            slant = total([v * h for v, h in zip(gained, hats)])
            inv = rs[now, at_rows, :]
            for g in range(groups):
                gmix = inv * (gained[g] - mean - hats[g] * slant)
                acc_small[taps, :, span[g]] += fold8(gmix)
                gm[g, pl.ds(base + PAD, rows_each), :] = gmix

        def finish(base):
            at_rows = pl.ds(base, rows_each)
            for g in range(groups):
                o = raw[at_rows, span[g]] + row(obias, g)
                dy = dy_ref[0, at_rows, span[g]].astype(F32)
                acc_small[scale, :, span[g]] += fold8(dy * o)
                acc_small[obias, :, span[g]] += fold8(dy)
                x = xp[now, g, pl.ds(base + PAD, rows_each), :]
                out_ref[0, at_rows, span[g]] = (x + o * row(scale, g)).astype(BF16)

        def conv_back(base):
            at_rows = pl.ds(base, rows_each)
            for g in range(groups):
                x = xp[now, g, pl.ds(base + PAD, rows_each), :]
                grad = dy_ref[0, at_rows, span[g]].astype(F32)
                for k in range(taps):
                    moved = gm[g, pl.ds(base + (PAD + margin - k), rows_each), :]
                    grad = grad + moved * row(k, g)
                    acc_small[k, :, span[g]] += fold8(moved * x)
                gx_ref[0, at_rows, span[g]] = grad.astype(BF16)

        def weights(unit):
            side, place = unit % 2, unit // 2
            cols = slice(place * hid_chunk, (place + 1) * hid_chunk)
            tall = chans + ONES * side
            acc[side, 0:tall, cols] += dot_nn(left[now, side, 0:tall], acts[side, :, cols])

        done = 0
        for i in range(parts):
            upto = units * (i + 1) // parts
            norm_back(i * rows_each)
            for unit in range(done, upto):
                weights(unit)
            done = upto
            finish(i * rows_each)
            if i > 0:
                conv_back((i - 1) * rows_each)
        conv_back(frames - rows_each)

    @pl.when(step == pl.num_programs(0) - 1)
    def _():
        gin_ref[...] = acc[1, 0:chans].astype(gin_ref.dtype)
        for j in range(0, hid, 128):
            gout_ref[j : j + 128, :] = acc[0, 0:chans, j : j + 128].T.astype(gout_ref.dtype)
        bias = acc[1, chans : chans + 8, :] * 0.125
        for g in range(groups):
            acc_small[obias, :, span[g]] *= row(scale, g)
        pack_small(acc_small, bias, rows_ref, small_ref)


def clip_call(counts, order, x, dy, w_in, w_out, pieces, taps, grad_dtype=BF16):
    clips, frames, chans = x.shape
    hid = w_in.shape[1]
    kinds = taps + 5

    def clip_spec(ahead):
        def index(i, counts, order):
            return order[jnp.minimum(i + ahead, clips - 1)], 0, 0

        return pl.BlockSpec((1, frames, chans), index)

    def whole(shape):
        return pl.BlockSpec(shape, lambda i, counts, order: (0,) * len(shape), pipeline_mode=pl.Buffered(1))

    groups = chans // 128
    return pl.pallas_call(
        partial(clip_kernel, taps=taps, hid_chunk=256, row_chunk=32, parts=8),
        out_shape=(
            jax.ShapeDtypeStruct(x.shape, BF16),
            jax.ShapeDtypeStruct(x.shape, BF16),
            jax.ShapeDtypeStruct((chans, hid), grad_dtype),
            jax.ShapeDtypeStruct((hid, chans), grad_dtype),
            jax.ShapeDtypeStruct(pieces.shape, F32),
        ),
        grid_spec=pltpu.PrefetchScalarGridSpec(
            num_scalar_prefetch=2,
            grid=(clips,),
            in_specs=[
                clip_spec(0),
                clip_spec(0),
                clip_spec(1),
                clip_spec(1),
                whole((chans, hid)),
                whole((hid, chans)),
                whole(pieces.shape),
            ],
            out_specs=(
                clip_spec(0),
                clip_spec(0),
                whole((chans, hid)),
                whole((hid, chans)),
                whole(pieces.shape),
            ),
            scratch_shapes=[
                pltpu.VMEM((16, chans), F32),
                pltpu.VMEM((8, hid), F32),
                pltpu.VMEM((2, groups, frames + 2 * PAD, 128), F32),
                pltpu.VMEM((groups, frames + 2 * PAD, 128), F32),
                pltpu.VMEM((2, groups, frames, 128), F32),
                pltpu.VMEM((2, frames, 128), F32),
                pltpu.VMEM((2, 2, chans + ONES, frames), BF16),
                pltpu.VMEM((2, frames, hid), BF16),
                pltpu.VMEM((2, frames, chans), BF16),
                pltpu.VMEM((2, frames, chans), BF16),
                pltpu.VMEM((frames, chans), F32),
                pltpu.VMEM((frames, chans), F32),
                pltpu.VMEM((2, chans + ONES, hid), F32),
                pltpu.VMEM((kinds, 8, chans), F32),
            ],
        ),
        compiler_params=pltpu.CompilerParams(vmem_limit_bytes=60 << 20),
        name="clips",
    )(counts, order, x, dy, x, dy, w_in, w_out, pieces)


MESH = pl.DeviceIdType.MESH


def grid_of(mesh_shape):
    across = mesh_shape["dp"] // 2
    deep = mesh_shape["fsdp"]
    tall = across if deep % across == 0 else 1
    return across, tall, deep // tall


def place(sizes):
    dp = lax.axis_index("dp")
    fsdp = lax.axis_index("fsdp")
    return dp // 2, dp % 2, fsdp // sizes[1], fsdp % sizes[1]


def at(sizes, x, core, z, y):
    return {"dp": x * 2 + core, "fsdp": z * sizes[1] + y}


def partners(sizes):
    x, core, z, y = place(sizes)
    across, tall, deep = sizes
    found = [at(sizes, x, 1 - core, z, y)]
    found += [at(sizes, (x + o) % across, core, z, y) for o in range(1, across)]
    found += [at(sizes, x, core, z, (y + o) % tall) for o in range(1, tall)]
    found += [at(sizes, x, core, (z + o) % deep, y) for o in range(1, deep)]
    return found


def greet(sizes):
    barrier = pltpu.get_barrier_semaphore()
    others = partners(sizes)
    for other in others:
        pl.semaphore_signal(barrier, inc=1, device_id=other, device_id_type=MESH)
    pl.semaphore_wait(barrier, len(others))


def send(src, dst, send_sems, recv_sems, slot, device):
    copy = pltpu.make_async_remote_copy(
        src_ref=src,
        dst_ref=dst,
        send_sem=send_sems.at[slot],
        recv_sem=recv_sems.at[slot],
        device_id=device,
        device_id_type=MESH,
    )
    copy.start()
    return copy


class Slots:
    def __init__(self):
        self.used = 0

    def take(self):
        self.used += 1
        return self.used - 1


def streams_of(refs_in, refs_full, cuts):
    widths = [r.shape[-1] for r in refs_in]
    found = [[(0, slice(0, widths[0]), True)]] + [[] for _ in range(cuts - 1)]
    for c in range(cuts):
        for i, x_first in ((1, True), (2, False)):
            each = widths[i] // cuts
            found[c].append((i, slice(c * each, (c + 1) * each), x_first))
    return found


def copies_of(sizes, streams):
    across, tall, deep = sizes
    columns = across * tall
    return streams * ((deep - 1) + (columns - 1) + columns)


def gather_kernel(*refs, sizes, cuts, slots, kinds):
    across, tall, deep = sizes
    counts_ref, conv_ref = refs[0:2]
    vectors = refs[2:7]
    bias_ref, in_ref, out_ref, full_small, full_in, full_out, order_ref = refs[7:14]
    tile, small_ref, send_sems, recv_sems, local_sems = refs[14:]
    x, core, z, y = place(sizes)
    slots_used = Slots()
    started = []
    greet(sizes)
    tile[...] = jnp.zeros_like(tile)
    taps, shard = conv_ref.shape
    tile[0:taps, 0:shard] = conv_ref[...].astype(F32)
    for k, vector in enumerate(vectors):
        tile[taps + k : taps + k + 1, 0:shard] = vector[...].astype(F32)
    tile[kinds : kinds + 1, 0 : bias_ref.shape[1]] = bias_ref[...].astype(F32)
    small_ref[...] = tile[...].astype(BF16)

    own = (small_ref, in_ref, out_ref)
    full = (full_small, full_in, full_out)
    groups = streams_of(own, full, cuts)

    def move(src, dst, device):
        copy = send(src, dst, send_sems, recv_sems, slots_used.take(), device)
        started.append(copy)
        return copy

    def column(stream, cx, cy):
        i, cols, _ = stream
        return full[i].at[cx, core, :, cy, :, cols]

    def along(stream, cx, cy, device):
        ref = column(stream, cx, cy)
        return move(ref, ref, device)

    def beside(stream, cx, cy):
        sides.append(along(stream, cx, cy, at(sizes, x, 1 - core, z, y)))

    keeps = []
    lines = {}
    sides = []
    for i in (1, 2, 0):
        keep = pltpu.make_async_copy(own[i], full[i].at[x, core, z, y], local_sems.at[i])
        keep.start()
        keeps.append(keep)
    for c in range(cuts):
        for s, (i, cols, _) in enumerate(groups[c]):
            lines[c, s] = [
                move(
                    own[i].at[:, cols],
                    full[i].at[x, core, z, y, :, cols],
                    at(sizes, x, core, (z + o) % deep, y),
                )
                for o in range(1, deep)
            ]
    for k in range(order_ref.shape[0]):
        order_ref[k] = clip_of(jnp.int32(k), counts_ref, slots)
    for keep in keeps:
        keep.wait()
    firsts = {}
    for c in range(cuts):
        for s, stream in enumerate(groups[c]):
            for copy in lines[c, s]:
                copy.wait_recv()
            firsts[c, s] = (
                [along(stream, x, y, at(sizes, (x + o) % across, core, z, y)) for o in range(1, across)],
                [along(stream, x, y, at(sizes, x, core, z, (y + o) % tall)) for o in range(1, tall)],
            )
            beside(stream, x, y)
    passed = {}
    for c in range(cuts):
        for s, stream in enumerate(groups[c]):
            along_x, along_y = firsts[c, s]
            lead, other = (along_x, along_y) if stream[2] else (along_y, along_x)
            passed[c, s] = []
            for o, copy in enumerate(lead, 1):
                copy.wait_recv()
                if stream[2]:
                    cx, cy = (x - o + across) % across, y
                    goals = [at(sizes, x, core, z, (y + p) % tall) for p in range(1, tall)]
                else:
                    cx, cy = x, (y - o + tall) % tall
                    goals = [at(sizes, (x + p) % across, core, z, y) for p in range(1, across)]
                passed[c, s].append([along(stream, cx, cy, goal) for goal in goals])
                beside(stream, cx, cy)
            for o, copy in enumerate(other, 1):
                copy.wait_recv()
                if stream[2]:
                    beside(stream, x, (y - o + tall) % tall)
                else:
                    beside(stream, (x - o + across) % across, y)
    for c in range(cuts):
        for s, stream in enumerate(groups[c]):
            for o, goals in enumerate(passed[c, s], 1):
                for p, copy in enumerate(goals, 1):
                    copy.wait_recv()
                    dx, dy = (o, p) if stream[2] else (p, o)
                    beside(stream, (x - dx + across) % across, (y - dy + tall) % tall)
    for copy in sides:
        copy.wait_recv()
    for copy in started:
        copy.wait_send()


def gather_call(sizes, counts, clips, conv, vectors, bias, w_in, w_out):
    across, tall, deep = sizes
    cuts = 2
    copies = copies_of(sizes, 2 * cuts + 1)
    vmem = pl.BlockSpec(memory_space=pltpu.VMEM)
    smem = pl.BlockSpec(memory_space=pltpu.SMEM)
    shapes = ((16, 128), w_in.shape, w_out.shape)
    kinds = conv.shape[0] + len(vectors)
    return pl.pallas_call(
        partial(gather_kernel, sizes=sizes, cuts=cuts, slots=clips // counts.shape[0], kinds=kinds),
        out_shape=tuple(jax.ShapeDtypeStruct((across, 2, deep, tall) + s, BF16) for s in shapes)
        + (jax.ShapeDtypeStruct((clips,), jnp.int32),),
        in_specs=[smem] + [vmem] * (len(vectors) + 4),
        out_specs=(pl.BlockSpec(memory_space=pl.ANY),) * 3 + (smem,),
        scratch_shapes=[
            pltpu.VMEM((16, 128), F32),
            pltpu.VMEM((16, 128), BF16),
            pltpu.SemaphoreType.DMA((copies,)),
            pltpu.SemaphoreType.DMA((copies,)),
            pltpu.SemaphoreType.DMA((3,)),
        ],
        compiler_params=pltpu.CompilerParams(collective_id=0, has_side_effects=True),
        name="gather",
    )(counts, conv, *vectors, bias, w_in, w_out)


def add_into(dst, terms):
    def block(k, carry):
        total = terms[0][k].astype(F32)
        for term in terms[1:]:
            total = total + term[k].astype(F32)
        dst[k] = total.astype(dst.dtype)
        return carry

    lax.fori_loop(0, dst.shape[0], block, 0)


def scatter_kernel(*refs, sizes, cuts):
    across, tall, deep = sizes
    parts = refs[0:3]
    outs = refs[3:6]
    side = refs[6:9]
    held = refs[9:12]
    corner = refs[12:15]
    mixed = refs[15:18]
    direct = refs[18:21]
    routed = refs[21:24]
    total = refs[24:27]
    lines = refs[27:30]
    send_sems, recv_sems = refs[30:32]
    x, core, z, y = place(sizes)
    slots_used = Slots()
    greet(sizes)
    started = []
    groups = streams_of(parts, outs, cuts)

    def move(src, dst, device):
        copy = send(src, dst, send_sems, recv_sems, slots_used.take(), device)
        started.append(copy)
        return copy

    def far(stream, a, b):
        if stream[2]:
            return (x + a) % across, (y + b) % tall
        return (x + b) % across, (y + a) % tall

    def lengths(stream):
        return (across, tall) if stream[2] else (tall, across)

    def peer(stream, a, b):
        cx, cy = far(stream, a, b)
        return at(sizes, cx, core, z, cy)

    def of(group, stream, *index):
        i, cols, _ = stream
        return group[i].at[index + (slice(None), slice(None), cols)]

    crossings = {}

    def cross(c, s, a, b):
        stream = groups[c][s]
        cx, cy = far(stream, a, b)
        i, cols, _ = stream
        crossings[c, s, a, b] = move(
            parts[i].at[cx, 1 - core, :, cy, :, cols],
            of(side, stream, cx, cy),
            at(sizes, x, 1 - core, z, y),
        )

    every = [(c, s) for c in range(cuts) for s in range(len(groups[c]))]
    for c in range(cuts):
        for kind in range(4):
            for s, stream in enumerate(groups[c]):
                last, first = lengths(stream)
                if kind == 0:
                    steps = [(a, b) for a in range(1, last) for b in range(1, first)]
                elif kind == 1:
                    steps = [(0, b) for b in range(1, first)]
                elif kind == 2:
                    steps = [(a, 0) for a in range(1, last)]
                else:
                    steps = [(0, 0)]
                for a, b in steps:
                    cross(c, s, a, b)

    def own(c, s, a, b):
        stream = groups[c][s]
        i, cols, _ = stream
        cx, cy = far(stream, a, b)
        crossings[c, s, a, b].wait_recv()
        add_into(of(held, stream, cx, cy), [parts[i].at[cx, core, :, cy, :, cols], of(side, stream, cx, cy)])
        return of(held, stream, cx, cy)

    corners, directs, routeds, ends = {}, {}, {}, {}

    def send_corners(c):
        for s, stream in enumerate(groups[c]):
            last, first = lengths(stream)
            for a in range(1, last):
                for b in range(1, first):
                    src = own(c, s, a, b)
                    corners[c, s, a, b] = move(src, of(corner, stream, a - 1, b - 1), peer(stream, 0, b))

    def send_directs(c):
        for s, stream in enumerate(groups[c]):
            for b in range(1, lengths(stream)[1]):
                src = own(c, s, 0, b)
                directs[c, s, b] = move(src, of(direct, stream, b - 1), peer(stream, 0, b))

    def send_routeds(c):
        for s, stream in enumerate(groups[c]):
            last, first = lengths(stream)
            for a in range(1, last):
                terms = [own(c, s, a, 0)]
                for b in range(1, first):
                    corners[c, s, a, b].wait_recv()
                    terms.append(of(corner, stream, a - 1, b - 1))
                add_into(of(mixed, stream, a - 1), terms)
                routeds[c, s, a] = move(of(mixed, stream, a - 1), of(routed, stream, a - 1), peer(stream, a, 0))

    def send_ends(c):
        for s, stream in enumerate(groups[c]):
            i, cols, _ = stream
            last, first = lengths(stream)
            terms = [own(c, s, 0, 0)]
            for b in range(1, first):
                directs[c, s, b].wait_recv()
                terms.append(of(direct, stream, b - 1))
            for a in range(1, last):
                routeds[c, s, a].wait_recv()
                terms.append(of(routed, stream, a - 1))
            add_into(of(total, stream), terms)
            for o in range(1, deep):
                ends[c, s, o] = move(
                    total[i].at[(z + o) % deep, :, cols],
                    lines[i].at[o - 1, :, cols],
                    at(sizes, x, core, (z + o) % deep, y),
                )

    send_corners(0)
    send_directs(0)
    for c in range(1, cuts):
        send_corners(c)
        send_routeds(c - 1)
        send_directs(c)
    send_routeds(cuts - 1)
    for c in range(cuts):
        send_ends(c)
    for c, s in every:
        i, cols, _ = groups[c][s]
        value = total[i][z, :, cols].astype(F32)
        for o in range(1, deep):
            ends[c, s, o].wait_recv()
            value = value + lines[i][o - 1, :, cols].astype(F32)
        outs[i][:, cols] = value
    for copy in started:
        copy.wait_send()


def scatter_call(sizes, small, g_in, g_out):
    across, tall, deep = sizes
    cuts = 2
    copies = copies_of(sizes, 2 * cuts + 1)
    parts = (small, g_in, g_out)
    vmem = pl.BlockSpec(memory_space=pltpu.VMEM)
    pieces = [p.shape[4:] for p in parts]
    kinds = [p.dtype for p in parts]

    def scratch(lead):
        return [pltpu.VMEM(lead(i) + pieces[i], kinds[i]) for i in range(3)]

    last = (across, across, tall)
    first = (tall, tall, across)
    grid = lambda i: (across, tall, deep)
    return pl.pallas_call(
        partial(scatter_kernel, sizes=sizes, cuts=cuts),
        out_shape=tuple(jax.ShapeDtypeStruct(p, F32) for p in pieces),
        in_specs=[vmem] * 3,
        out_specs=(vmem,) * 3,
        scratch_shapes=[
            *scratch(grid),
            *scratch(grid),
            *scratch(lambda i: (max(last[i] - 1, 1), max(first[i] - 1, 1), deep)),
            *scratch(lambda i: (max(last[i] - 1, 1), deep)),
            *scratch(lambda i: (max(first[i] - 1, 1), deep)),
            *scratch(lambda i: (max(last[i] - 1, 1), deep)),
            *scratch(lambda i: (deep,)),
            *scratch(lambda i: (max(deep - 1, 1),)),
            pltpu.SemaphoreType.DMA((copies,)),
            pltpu.SemaphoreType.DMA((copies,)),
        ],
        compiler_params=pltpu.CompilerParams(collective_id=1, has_side_effects=True, vmem_limit_bytes=60 << 20),
        name="scatter",
    )(*parts)


def close_kernel(small_ref, in_ref, out_ref, *results, taps):
    conv, bias, g_in, g_out = results[0], results[6], results[7], results[8]
    shard = conv.shape[1]
    conv[...] = small_ref[0:taps, 0:shard]
    for k in range(5):
        results[1 + k][...] = small_ref[taps + k : taps + k + 1, 0:shard]
    bias[...] = small_ref[taps + 5 : taps + 6, 0 : bias.shape[1]]
    g_in[...] = in_ref[...]
    g_out[...] = out_ref[...]


def close_call(small, g_in, g_out, taps, shard, wide):
    shapes = [(taps, shard)] + [(1, shard)] * 5 + [(1, wide), g_in.shape, g_out.shape]
    return pl.pallas_call(
        partial(close_kernel, taps=taps),
        out_shape=tuple(jax.ShapeDtypeStruct(s, F32) for s in shapes),
        name="close",
    )(small, g_in, g_out)


def on_device(
    mel_clips,
    live_counts,
    conv_weight,
    conv_bias,
    norm_gain,
    norm_shift,
    in_weight,
    in_bias,
    out_weight,
    out_bias,
    layer_scale,
    cotangent,
    *,
    sizes,
):
    shard, taps = conv_weight.shape
    hid = in_weight.shape[1]
    devices = lax.axis_size(("dp", "fsdp"))
    chans = shard * devices
    wide = in_bias.shape[0]
    lead = (sizes[0], 2, sizes[2], sizes[1])

    counts = live_counts.reshape(-1)
    vectors = [v[None, :] for v in (conv_bias, norm_gain, norm_shift, out_bias, layer_scale)]
    small, full_in, full_out, order = gather_call(
        sizes, counts, mel_clips.shape[0], conv_weight.T, vectors, in_bias[None, :], in_weight, out_weight
    )
    block_out, grad_clips, grad_in, grad_out, small = clip_call(
        counts,
        order,
        mel_clips,
        cotangent,
        full_in.reshape(chans, hid),
        full_out.reshape(hid, chans),
        small.reshape(devices, 16, 128),
        taps,
    )
    small, grad_in, grad_out = scatter_call(
        sizes,
        small.reshape(lead + (16, 128)),
        grad_in.reshape(lead + in_weight.shape),
        grad_out.reshape(lead + out_weight.shape),
    )
    conv, cbias, gain, shift, obias, scale, ibias, grad_in, grad_out = close_call(
        small, grad_in, grad_out, taps, shard, wide
    )
    vector = lambda v: v.reshape(-1)
    return (
        block_out,
        grad_clips,
        conv.T,
        vector(cbias),
        vector(gain),
        vector(shift),
        grad_in,
        vector(ibias),
        grad_out,
        vector(obias),
        vector(scale),
    )


def solution(mesh):
    both = ("dp", "fsdp")
    row, mat, cube = P(both), P(both, None), P(both, None, None)
    in_specs = (cube, mat, mat, row, row, row, mat, row, mat, row, row, cube)
    out_specs = (cube, cube, mat, row, row, row, mat, row, mat, row, row)
    body = partial(on_device, sizes=grid_of(mesh.shape))
    return jax.shard_map(body, mesh=mesh, in_specs=in_specs, out_specs=out_specs, check_vma=False)
```
